256 devices in a mesh: grp: 16 (over x, y_lo, core), inner: 16 (over y_hi, z).
Axes of the slice: x: 4, y: 4 (y_hi: 2, y_lo: 2; y = y_hi * 2 + y_lo), z: 8, core: 2. Of those that a mesh axis runs over, the one named last changes fastest.
Arguments:
- amplitudes: bfloat16 [32, 8, 12288], P('grp', None, 'inner'), may hold values from -6 to 6
- factors: bfloat16 [32, 2000, 12288], P('grp', 'inner'), may hold values from -0.125 to 0.125
- atom_charges: bfloat16 [32, 64, 12288], P('grp', None, 'inner'), may hold values from -0.0068359375 to 0.0068359375
- eps_occ: float32 [32, 48], P('grp'), may hold values from -1.2 to -0.3
- eps_vir: float32 [32, 256], P('grp'), may hold values from 0.1 to 1.5
- occ_count: int32 [32], P('grp'), may hold values from 24 to 48
- vir_count: int32 [32], P('grp'), may hold values from 128 to 256
- atom_list: int32 [2048], P('grp'), may hold values from 0 to 2047, each once
- positions: float32 [3, 2048], replicated, may hold values from 0 to 12
Outputs:
- refined: float32 [32, 8, 12288], P('grp', None, 'inner')
- hamiltonian: float32 [256, 16, 16], P('grp', None, 'inner')
The draws below stay inside these ranges and needn't reach their ends.
Inputs may be any that keep to these rules, and one draw needn't show every extreme that they name: `atom_list`: every atom index appears exactly once.
All inputs are finite; a program needn't handle non-finite values.
Results may differ from the reference program's by a relative error of at most 0.022.
Values may be sent and summed in bfloat16 or wider, within the bound.
A program may use at most 64 MiB of HBM per device.

```python
import functools
import jax
import jax.numpy as jnp
from jax import lax

NOCC = 48
NVIR = 256
NAUX = 2000
STATES = 8
ATOMS = 64
OV = 12288
CHROMOPHORES = 32
ALL_ATOMS = 2048
GSTATES = 16
NSTATE = 256
N_GRP = 16
N_INNER = 16


def place_ends(drawn, stream_key, low, largest):
    longest = drawn.shape.index(max(drawn.shape))
    spots = []
    for shift in (0, 1):
        where = [jax.random.randint(jax.random.fold_in(stream_key, axis), (), 0, length) for axis, length in enumerate(drawn.shape)]
        where[longest] = (where[longest] + shift) % drawn.shape[longest]
        spots.append(tuple(where))
    return drawn.at[spots[0]].set(low).at[spots[1]].set(largest)


def block_levels(rng, dims, shards, smallest, largest):
    gain, own = 1.0, jax.random.fold_in(rng, 6)
    for position, parts in shards:
        draws = jnp.exp(jax.random.uniform(jax.random.fold_in(own, position), (parts,), jnp.float32, smallest / len(shards), largest / len(shards)))
        gain = gain * jnp.repeat(draws, dims[position] // parts).reshape([-1 if axis == position else 1 for axis in range(len(dims))])
    return gain


def bell_draw(stream_key, extent, width, most, cuts=(), held_as=jnp.bfloat16):
    entries = width * jax.random.normal(stream_key, extent, jnp.float32)
    if cuts:
        entries = entries * block_levels(stream_key, extent, cuts, -0.22, 0.18)
    return jnp.clip(entries, -most, most).astype(held_as)


def setup_inputs(seed: int = 0) -> dict:
    arg_keys = jax.random.split(jax.random.key(seed), 10)
    amplitudes = bell_draw(arg_keys[0], (CHROMOPHORES, STATES, OV), 1.0, 6.0, ((0, 16), (2, 16)))
    factors = bell_draw(arg_keys[1], (CHROMOPHORES, NAUX, OV), NAUX ** -0.5, 0.125, ((0, 16), (1, 16)))
    atom_charges = bell_draw(arg_keys[2], (CHROMOPHORES, ATOMS, OV), (OV * ATOMS) ** -0.5, 0.0068359375, ((0, 16), (2, 16)))
    eps_occ = jnp.clip(-1.2 + 0.90000004 * jax.random.uniform(arg_keys[3], (CHROMOPHORES, NOCC), jnp.float32) ** block_levels(arg_keys[3], (CHROMOPHORES, NOCC), ((0, 16),), -0.2, 0.2), -1.2, -0.3)
    eps_vir = jnp.clip(0.1 + 1.4 * jax.random.uniform(arg_keys[4], (CHROMOPHORES, NVIR), jnp.float32) ** block_levels(arg_keys[4], (CHROMOPHORES, NVIR), ((0, 16),), -0.2, 0.2), 0.1, 1.5)
    occ_count = place_ends(jax.random.randint(arg_keys[5], (CHROMOPHORES,), NOCC // 2, NOCC + 1), jax.random.fold_in(arg_keys[5], 1), NOCC // 2, NOCC).astype(jnp.int32)
    vir_count = place_ends(jax.random.randint(arg_keys[6], (CHROMOPHORES,), NVIR // 2, NVIR + 1), jax.random.fold_in(arg_keys[6], 1), NVIR // 2, NVIR).astype(jnp.int32)
    atom_list = jax.random.permutation(arg_keys[7], ALL_ATOMS).astype(jnp.int32)
    positions = jnp.clip(jax.random.uniform(arg_keys[8], (3, ALL_ATOMS), jnp.float32, 0.0, 12.0), 0.0, 12.0)
    return {"amplitudes": amplitudes, "factors": factors, "atom_charges": atom_charges, "eps_occ": eps_occ, "eps_vir": eps_vir, "occ_count": occ_count, "vir_count": vir_count, "atom_list": atom_list, "positions": positions}


epsilon = 1e-06

def monomer(packed):
    factor, current, charge_map, occ_energy, vir_energy, occ_limit, vir_limit = packed
    pair_index = jnp.arange(OV, dtype=jnp.int32)
    occ_of = pair_index // NVIR
    vir_of = pair_index % NVIR
    active = ((occ_of < occ_limit) & (vir_of < vir_limit)).astype(jnp.float32)
    gap = vir_energy[vir_of] - occ_energy[occ_of]
    masked = current * active.astype(jnp.bfloat16)[None, :]
    fitted = jnp.dot(masked, factor.T, preferred_element_type=jnp.float32)
    fitted_low = fitted.astype(jnp.bfloat16)
    block_aux = NAUX // N_INNER
    fitted_blocks = fitted_low.astype(jnp.float32).reshape(STATES, N_INNER, block_aux)
    factor_blocks = factor.astype(jnp.float32).reshape(N_INNER, block_aux, OV)
    partial_value = 2.0 * jnp.einsum('sja,jao->jso', fitted_blocks, factor_blocks)
    coulomb = lax.optimization_barrier(jnp.sum(partial_value.astype(jnp.bfloat16).astype(jnp.float32), axis=0))
    start = masked.astype(jnp.float32)
    image = gap[None, :] * start + coulomb * active[None, :]
    energies = lax.optimization_barrier(jnp.sum(start * image, axis=1)) / (lax.optimization_barrier(jnp.sum(start * start, axis=1)) + epsilon)
    refined = active[None, :] * (start - (image - energies[:, None] * start) / gap[None, :])
    charges = jnp.dot(refined.astype(jnp.bfloat16), charge_map.T, preferred_element_type=jnp.float32)
    return (refined, charges, energies)

def coupling_rows(packed, xyz_all, charges_all):
    own_xyz, own_charges, own_energy, which = packed
    offset = own_xyz[:, :, None, None] - jnp.transpose(xyz_all, (1, 0, 2))[:, None, :, :]
    kernel = 1.0 / jnp.sqrt(lax.optimization_barrier(jnp.sum(offset * offset, axis=0)) + 1.0)
    block = jnp.einsum('sa,adb,dtb->sdt', own_charges, kernel, charges_all, precision=lax.Precision.HIGHEST)
    same = (jnp.arange(CHROMOPHORES, dtype=jnp.int32) == which)[None, :, None]
    diagonal = jnp.eye(STATES, dtype=jnp.float32)[:, None, :] * own_energy[:, None, None]
    return jnp.where(same, diagonal, block)

def reference(amplitudes, factors, atom_charges, eps_occ, eps_vir, occ_count, vir_count, atom_list, positions):
    refined, charges, energies = lax.map(monomer, (factors, amplitudes, atom_charges, eps_occ, eps_vir, occ_count, vir_count))
    coords = jnp.take(positions, atom_list, axis=1).reshape(3, CHROMOPHORES, ATOMS).transpose(1, 0, 2)
    which = jnp.arange(CHROMOPHORES, dtype=jnp.int32)
    blocks = lax.map(functools.partial(coupling_rows, xyz_all=coords, charges_all=charges), (coords, charges, energies, which))
    return (refined, blocks.reshape(NSTATE, N_GRP, GSTATES))
```

```python
import functools

import jax
import jax.numpy as jnp
from jax import lax
from jax.experimental import pallas as pl
from jax.experimental.pallas import tpu as pltpu
from jax.sharding import PartitionSpec as P

NVIR = 256
STATES = 8
EPSILON = 1e-06
Z = 8
MESH = pl.DeviceIdType.MESH
PEERS = sorted(
    [(dy, dz) for dy in (0, 1) for dz in range(Z) if (dy, dz) != (0, 0)],
    key=lambda r: -(2 * r[0] + min(r[1], Z - r[1])),
)
N_IN = len(PEERS)
N_GRP = 15
NT = (((1,), (1,)), ((), ()))
NN = (((1,), (0,)), ((), ()))


def split(x):
    high = x.astype(jnp.bfloat16)
    return high, (x - high.astype(jnp.float32)).astype(jnp.bfloat16)


def dot(a, b, dims):
    return lax.dot_general(a, b, dims, preferred_element_type=jnp.float32)


def inner_at(rel, sign):
    me = lax.axis_index("inner")
    y, z = me // Z, me % Z
    return lax.rem(y + rel[0], 2) * Z + lax.rem(z + sign * rel[1] + Z, Z)


def grp_at(step, sign):
    return lax.rem(lax.axis_index("grp") + sign * step + 16, 16)


def remote(src, dst, sems, n, axis, where):
    return pltpu.make_async_remote_copy(
        src_ref=src,
        dst_ref=dst,
        send_sem=sems.at[0, n],
        recv_sem=sems.at[1, n],
        device_id={axis: where},
        device_id_type=MESH,
    )


def kernel(
    amp_ref, fac_hbm, chg_ref, occ_e, vir_e, occ_n, vir_n, atoms_ref, pos_ref,
    refined_ref, block_ref,
    fac, amp_land, part, part_land, e_send, e_land, c_send, c_land, g_send, g_land, x_send, x_land,
    pos8, k_hi, k_lo, fac_sem, amp_sem, part_sem, e_sem, c_sem, g_sem, x_sem,
):
    me = lax.axis_index("inner")
    grp = lax.axis_index("grp")
    rows_n, pairs = amp_ref.shape
    segs = pairs // NVIR
    aux, tiles = fac_hbm.shape[:2]

    barrier = pltpu.get_barrier_semaphore()
    for rel in PEERS:
        pl.semaphore_signal(barrier, inc=1, device_id={"inner": inner_at(rel, 1)}, device_id_type=MESH)
    for a in range(1, 16):
        pl.semaphore_signal(barrier, inc=1, device_id={"grp": grp_at(a, 1)}, device_id_type=MESH)
    loads = []
    for j in range(tiles):
        fac[j, aux:128] = jnp.zeros((128 - aux, 2, 128), jnp.bfloat16)
        loads.append(pltpu.make_async_copy(fac_hbm.at[:, j], fac.at[j, pl.ds(0, aux)], fac_sem))
        loads[-1].start()
    flat = fac.reshape(tiles, 256, 128)
    per = pairs // 128

    def piece(who):
        return jnp.concatenate([flat[who * per + m] for m in range(per)], axis=1)

    pos8[...] = jnp.zeros_like(pos8)
    pos8[0:3, :] = pos_ref[...]
    p_all = pos8[...]
    p_hi = p_all.astype(jnp.bfloat16)
    rest = p_all - p_hi.astype(jnp.float32)
    p_mid = rest.astype(jnp.bfloat16)
    p_lo = (rest - p_mid.astype(jnp.float32)).astype(jnp.bfloat16)
    table = pos_ref.shape[1]
    hot = (
        (lax.broadcasted_iota(jnp.int32, (table, 128), 0) == atoms_ref[...])
        .astype(jnp.float32)
        .astype(jnp.bfloat16)
    )
    own_xyz = dot(p_hi, hot, NN) + dot(p_mid, hot, NN) + dot(p_lo, hot, NN)
    x_send[...] = own_xyz

    pl.semaphore_wait(barrier, N_IN + N_GRP)

    amp_copies = [
        remote(amp_ref, amp_land.at[n], amp_sem, n, "inner", inner_at(rel, 1))
        for n, rel in enumerate(PEERS)
    ]
    for c in amp_copies:
        c.start()
    x_copies = [
        remote(x_send, x_land.at[a - 1], x_sem, a - 1, "grp", grp_at(a, 1)) for a in range(1, 16)
    ]
    for c in x_copies:
        c.start()

    lane = lax.broadcasted_iota(jnp.int32, (STATES, pairs), 1)
    seg, vir = lane // NVIR, lane % NVIR
    vir_in = [vir < vir_n[c] for c in range(2)]

    def active_of(who):
        return jnp.concatenate(
            [jnp.where(vir_in[c] & (seg + who * segs < occ_n[c]), 1.0, 0.0) for c in range(2)],
            axis=0,
        )

    active = active_of(me)
    gap = jnp.concatenate(
        [
            jnp.concatenate(
                [
                    jnp.broadcast_to(vir_e[c : c + 1, :] - occ_e[c, me * segs + m], (STATES, NVIR))
                    for m in range(segs)
                ],
                axis=1,
            )
            for c in range(2)
        ],
        axis=0,
    )
    masked = amp_ref[...].astype(jnp.float32) * active

    for c in loads:
        c.wait()

    fitted = dot(masked.astype(jnp.bfloat16), piece(me), NT)
    for n in reversed(range(N_IN)):
        amp_copies[n].wait_recv()
        who = inner_at(PEERS[n], -1)
        theirs = (amp_land[n].astype(jnp.float32) * active_of(who)).astype(jnp.bfloat16)
        fitted = fitted + dot(theirs, piece(who), NT)
    parity = lax.broadcasted_iota(jnp.int32, fitted.shape, 1) % 2
    monomer = lax.broadcasted_iota(jnp.int32, fitted.shape, 0) // STATES
    fitted = jnp.where(parity == monomer, fitted, 0.0)
    low = fitted.astype(jnp.bfloat16)

    row16 = lax.broadcasted_iota(jnp.int32, (rows_n, 128), 0)
    lane16 = lax.broadcasted_iota(jnp.int32, (rows_n, 128), 1)
    num = jnp.sum(gap * masked * masked, axis=1, keepdims=True) + 2.0 * jnp.sum(
        low.astype(jnp.float32) * fitted, axis=1, keepdims=True
    )
    sq = jnp.sum(masked * masked, axis=1, keepdims=True)
    tile = jnp.where(lane16 == row16, num, 0.0) + jnp.where(lane16 == row16 + 16, sq, 0.0)
    e_row = jnp.sum(tile, axis=0, keepdims=True)
    e_send[...] = e_row
    e_copies = [
        remote(e_send, e_land.at[n], e_sem, n, "inner", inner_at(rel, 1))
        for n, rel in enumerate(PEERS)
    ]
    for c in e_copies:
        c.start()

    part_copies = []
    for n, rel in enumerate(PEERS):
        who = inner_at(rel, 1)
        part[n] = (2.0 * dot(low, piece(who), NN)).astype(jnp.bfloat16)
        copy = remote(part.at[n], part_land.at[n], part_sem, n, "inner", who)
        copy.start()
        part_copies.append(copy)
    coulomb = (2.0 * dot(low, piece(me), NN)).astype(jnp.bfloat16).astype(jnp.float32)

    own_cols = jnp.transpose(own_xyz)
    for a in range(16):
        if a > 0:
            x_copies[a - 1].wait_recv()
        there = own_xyz if a == 0 else x_land[a - 1]
        r2 = jnp.zeros((128, 128), jnp.float32)
        for k in range(3):
            d = own_cols[:, k : k + 1] - there[k : k + 1, :]
            r2 = r2 + d * d
        hi, lo = split(lax.rsqrt(r2 + 1.0))
        k_hi[:, a * 128 : (a + 1) * 128] = hi
        k_lo[:, a * 128 : (a + 1) * 128] = lo

    for copy in e_copies:
        copy.wait_recv()
    total = e_row
    for n in range(N_IN):
        total = total + e_land[n]
    num = jnp.sum(jnp.where(lane16 == row16, total, 0.0), axis=1, keepdims=True)
    sq = jnp.sum(jnp.where(lane16 == row16 + 16, total, 0.0), axis=1, keepdims=True)
    energy = num / (sq + EPSILON)

    for n in reversed(range(N_IN)):
        part_copies[n].wait_recv()
        coulomb = coulomb + part_land[n].astype(jnp.float32)

    sigma = gap * masked + active * coulomb
    refined = active * (masked - (sigma - energy * masked) / gap)
    refined_ref[...] = refined
    both = dot(refined.astype(jnp.bfloat16), chg_ref[...], NT)
    first = lane16[0:STATES] < 64
    own = jnp.where(first, both[0:STATES], both[STATES:])
    c_send[...] = own
    c_copies = [
        remote(c_send, c_land.at[n], c_sem, n, "inner", inner_at(rel, 1))
        for n, rel in enumerate(PEERS)
    ]
    for c in c_copies:
        c.start()
    charges = own
    for n in reversed(range(N_IN)):
        c_copies[n].wait_recv()
        charges = charges + c_land[n]
    g_send[...] = charges
    g_copies = [
        remote(g_send, g_land.at[a - 1], g_sem, a - 1, "grp", grp_at(a, 1)) for a in range(1, 16)
    ]
    for c in g_copies:
        c.start()

    rows = jnp.concatenate([jnp.where(first, charges, 0.0), jnp.where(first, 0.0, charges)], axis=0)
    rows_hi, rows_lo = split(rows)
    with_hi = dot(jnp.concatenate([rows_hi, rows_lo], axis=0), k_hi[...], NN)
    field = with_hi[0:16] + with_hi[16:32] + dot(rows_hi, k_lo[...], NN)

    t = lax.rem(me, STATES)
    half = me // STATES
    in_half = (lax.broadcasted_iota(jnp.int32, (1, 128), 1) // 64) == half
    out_lane = lax.broadcasted_iota(jnp.int32, (16, 16), 1)
    block = jnp.zeros((16, 16), jnp.float32)
    for a in range(16):
        if a > 0:
            g_copies[a - 1].wait_recv()
        src = g_send if a == 0 else g_land.at[a - 1]
        q = jnp.where(in_half, src[pl.ds(t, 1), :], 0.0)
        column = jnp.sum(field[:, a * 128 : (a + 1) * 128] * q, axis=1, keepdims=True)
        block = jnp.where(out_lane == grp_at(a, -1), column, block)
    out_row = lax.broadcasted_iota(jnp.int32, (16, 16), 0)
    same = (out_lane == grp) & (out_row // STATES == half)
    block_ref[...] = jnp.where(same, jnp.where(out_row % STATES == t, energy, 0.0), block)

    for copies in (amp_copies, x_copies, e_copies, part_copies, c_copies, g_copies):
        for c in copies:
            c.wait_send()


def local(
    amplitudes, factors, atom_charges, eps_occ, eps_vir, occ_count, vir_count, atom_list, positions
):
    monomers, states, pairs = amplitudes.shape
    aux, every = factors.shape[1:]
    rows = monomers * states
    vmem = pl.BlockSpec(memory_space=pltpu.VMEM)
    smem = pl.BlockSpec(memory_space=pltpu.SMEM)
    bf, f32 = jnp.bfloat16, jnp.float32
    by_tile = jnp.transpose(factors, (1, 0, 2)).reshape(aux, monomers, every // 128, 128)
    refined, block = pl.pallas_call(
        kernel,
        name="exciton",
        out_shape=(
            jax.ShapeDtypeStruct((rows, pairs), f32),
            jax.ShapeDtypeStruct((rows, rows), f32),
        ),
        in_specs=[vmem, pl.BlockSpec(memory_space=pl.ANY), vmem, smem, vmem, smem, smem, vmem, vmem],
        out_specs=(vmem, vmem),
        scratch_shapes=[
            pltpu.VMEM((every // 128, 128, monomers, 128), bf),
            pltpu.VMEM((N_IN, rows, pairs), bf),
            pltpu.VMEM((N_IN, rows, pairs), bf),
            pltpu.VMEM((N_IN, rows, pairs), bf),
            pltpu.VMEM((1, 128), f32),
            pltpu.VMEM((N_IN, 1, 128), f32),
            pltpu.VMEM((8, 128), f32),
            pltpu.VMEM((N_IN, 8, 128), f32),
            pltpu.VMEM((8, 128), f32),
            pltpu.VMEM((N_GRP, 8, 128), f32),
            pltpu.VMEM((8, 128), f32),
            pltpu.VMEM((N_GRP, 8, 128), f32),
            pltpu.VMEM((8, positions.shape[1]), f32),
            pltpu.VMEM((128, 2048), bf),
            pltpu.VMEM((128, 2048), bf),
            pltpu.SemaphoreType.DMA,
        ]
        + [pltpu.SemaphoreType.DMA((2, 15))] * 6,
        compiler_params=pltpu.CompilerParams(collective_id=0, has_side_effects=True),
    )(
        amplitudes.reshape(rows, pairs),
        by_tile.transpose(0, 2, 1, 3),
        atom_charges.reshape(monomers * 64, pairs),
        eps_occ, eps_vir, occ_count, vir_count, atom_list.reshape(1, -1), positions,
    )
    return refined.reshape(monomers, states, pairs), block.reshape(rows, rows, 1)


def solution(mesh):
    in_specs = (
        P("grp", None, "inner"),
        P("grp", "inner", None),
        P("grp", None, "inner"),
        P("grp", None),
        P("grp", None),
        P("grp"),
        P("grp"),
        P("grp"),
        P(),
    )
    out_specs = (P("grp", None, "inner"), P("grp", None, "inner"))
    return jax.shard_map(local, mesh=mesh, in_specs=in_specs, out_specs=out_specs, check_vma=False)
```

```python
import jax
import jax.numpy as jnp
from jax import lax
from jax.experimental import pallas as pl
from jax.experimental.pallas import tpu as pltpu
from jax.sharding import PartitionSpec as P

NVIR = 256
STATES = 8
EPSILON = 1e-06
Z = 8
MESH = pl.DeviceIdType.MESH
FAR_Z = (4, 3, 5, 2, 6, 1, 7)
PEERS = sorted(
    [(dy, dz) for dy in (0, 1) for dz in range(Z) if (dy, dz) != (0, 0)],
    key=lambda r: -(2 * r[0] + min(r[1], Z - r[1])),
)
N_IN = len(PEERS)
N_Z = len(FAR_Z)
N_GRP = 15
NT = (((1,), (1,)), ((), ()))
NN = (((1,), (0,)), ((), ()))


def split(x):
    high = x.astype(jnp.bfloat16)
    return high, (x - high.astype(jnp.float32)).astype(jnp.bfloat16)


def dot(a, b, dims):
    return lax.dot_general(a, b, dims, preferred_element_type=jnp.float32)


def inner_at(rel, sign):
    me = lax.axis_index("inner")
    y, z = me // Z, me % Z
    return lax.rem(y + rel[0], 2) * Z + lax.rem(z + sign * rel[1] + Z, Z)


def grp_at(step, sign):
    return lax.rem(lax.axis_index("grp") + sign * step + 16, 16)


def remote(src, dst, sems, n, axis, where):
    return pltpu.make_async_remote_copy(
        src_ref=src,
        dst_ref=dst,
        send_sem=sems.at[0, n],
        recv_sem=sems.at[1, n],
        device_id={axis: where},
        device_id_type=MESH,
    )


def start_all(copies):
    for c in copies:
        c.start()
    return copies


def kernel(
    amp_hbm, fac_hbm, chg_hbm, occ_e_hbm, vir_e_hbm, occ_n_hbm, vir_n_hbm, atoms_hbm, pos_hbm,
    refined_ref, block_ref,
    amp_ref, chg_ref, occ_e, vir_e, occ_n, vir_n, atoms_ref, pos_ref,
    fac, amp_y, amp_z, amp_yz, part_y, land_y, part_z, land_z,
    e_send, e_land, c_send, c_land, g_send, g_land, x_send, x_land, pos8, k_hi, k_lo,
    in_sem, fac_sem, ay_sem, az_sem, ayz_sem, py_sem, pz_sem, e_sem, c_sem, g_sem, x_sem,
):
    me = lax.axis_index("inner")
    grp = lax.axis_index("grp")
    rows_n, pairs = amp_ref.shape
    segs = pairs // NVIR
    aux, tiles = fac_hbm.shape[:2]
    per = pairs // 128

    barrier = pltpu.get_barrier_semaphore()
    for rel in [(1, 0)] + [(0, dz) for dz in FAR_Z]:
        pl.semaphore_signal(barrier, inc=1, device_id={"inner": inner_at(rel, 1)}, device_id_type=MESH)
    for a in range(1, 16):
        pl.semaphore_signal(barrier, inc=1, device_id={"grp": grp_at(a, 1)}, device_id_type=MESH)
    pairs_in = [
        (amp_hbm, amp_ref), (vir_e_hbm, vir_e), (occ_e_hbm, occ_e), (occ_n_hbm, occ_n),
        (vir_n_hbm, vir_n), (atoms_hbm, atoms_ref), (pos_hbm, pos_ref), (chg_hbm, chg_ref),
    ]
    inputs = start_all(
        [pltpu.make_async_copy(src, dst, in_sem.at[n]) for n, (src, dst) in enumerate(pairs_in)]
    )
    inputs[0].wait()
    pl.semaphore_wait(barrier, 1 + N_Z + N_GRP)

    to_y = remote(amp_ref, amp_y, ay_sem, 0, "inner", inner_at((1, 0), 1))
    to_y.start()
    to_z = start_all(
        [
            remote(amp_ref, amp_z.at[n], az_sem, n, "inner", inner_at((0, dz), 1))
            for n, dz in enumerate(FAR_Z)
        ]
    )
    loads = []
    for j in range(tiles):
        loads.append(pltpu.make_async_copy(fac_hbm.at[:, j], fac.at[j, pl.ds(0, aux)], fac_sem))
        loads[-1].start()
    to_y.wait_recv()
    onward = start_all(
        [
            remote(amp_y, amp_yz.at[n], ayz_sem, n, "inner", inner_at((0, dz), 1))
            for n, dz in enumerate(FAR_Z)
        ]
    )
    for copy in inputs[1:]:
        copy.wait()
    for j in range(tiles):
        fac[j, aux:128] = jnp.zeros((128 - aux, 2, 128), jnp.bfloat16)
    flat = fac.reshape(tiles, 256, 128)

    def piece(who):
        return jnp.concatenate([flat[who * per + m] for m in range(per)], axis=1)

    pos8[...] = jnp.zeros_like(pos8)
    pos8[0:3, :] = pos_ref[...]
    p_all = pos8[...]
    p_hi = p_all.astype(jnp.bfloat16)
    rest = p_all - p_hi.astype(jnp.float32)
    p_mid = rest.astype(jnp.bfloat16)
    p_lo = (rest - p_mid.astype(jnp.float32)).astype(jnp.bfloat16)
    hot = (
        (lax.broadcasted_iota(jnp.int32, (pos_ref.shape[1], 128), 0) == atoms_ref[...])
        .astype(jnp.float32)
        .astype(jnp.bfloat16)
    )
    own_xyz = dot(p_hi, hot, NN) + dot(p_mid, hot, NN) + dot(p_lo, hot, NN)
    x_send[...] = own_xyz
    x_copies = start_all(
        [remote(x_send, x_land.at[a - 1], x_sem, a - 1, "grp", grp_at(a, 1)) for a in range(1, 16)]
    )

    lane = lax.broadcasted_iota(jnp.int32, (STATES, pairs), 1)
    seg, vir = lane // NVIR, lane % NVIR
    vir_in = [vir < vir_n[c] for c in range(2)]

    def active_of(who):
        return jnp.concatenate(
            [jnp.where(vir_in[c] & (seg + who * segs < occ_n[c]), 1.0, 0.0) for c in range(2)],
            axis=0,
        )

    active = active_of(me)
    gap = jnp.concatenate(
        [
            jnp.concatenate(
                [
                    jnp.broadcast_to(vir_e[c : c + 1, :] - occ_e[c, me * segs + m], (STATES, NVIR))
                    for m in range(segs)
                ],
                axis=1,
            )
            for c in range(2)
        ],
        axis=0,
    )
    masked = amp_ref[...].astype(jnp.float32) * active

    for c in loads:
        c.wait()

    def fit(amps, who):
        theirs = (amps.astype(jnp.float32) * active_of(who)).astype(jnp.bfloat16)
        return dot(theirs, piece(who), NT)

    fitted = dot(masked.astype(jnp.bfloat16), piece(me), NT)
    fitted = fitted + fit(amp_y[...], inner_at((1, 0), 1))
    for n in reversed(range(N_Z)):
        to_z[n].wait_recv()
        fitted = fitted + fit(amp_z[n], inner_at((0, FAR_Z[n]), -1))
    for n in reversed(range(N_Z)):
        onward[n].wait_recv()
        fitted = fitted + fit(amp_yz[n], inner_at((1, FAR_Z[n]), -1))
    parity = lax.broadcasted_iota(jnp.int32, fitted.shape, 1) % 2
    monomer = lax.broadcasted_iota(jnp.int32, fitted.shape, 0) // STATES
    fitted = jnp.where(parity == monomer, fitted, 0.0)
    low = fitted.astype(jnp.bfloat16)

    order = FAR_Z + (0,)
    cross = []
    for n, dz in enumerate(order):
        part_y[n] = (2.0 * dot(low, piece(inner_at((1, dz), 1)), NN)).astype(jnp.bfloat16)
        cross.append(remote(part_y.at[n], land_y.at[n], py_sem, n, "inner", inner_at((1, 0), 1)))
        cross[-1].start()

    row16 = lax.broadcasted_iota(jnp.int32, (rows_n, 128), 0)
    lane16 = lax.broadcasted_iota(jnp.int32, (rows_n, 128), 1)
    num = jnp.sum(gap * masked * masked, axis=1, keepdims=True) + 2.0 * jnp.sum(
        low.astype(jnp.float32) * fitted, axis=1, keepdims=True
    )
    sq = jnp.sum(masked * masked, axis=1, keepdims=True)
    tile = jnp.where(lane16 == row16, num, 0.0) + jnp.where(lane16 == row16 + 16, sq, 0.0)
    e_row = jnp.sum(tile, axis=0, keepdims=True)
    e_send[...] = e_row
    e_copies = start_all(
        [
            remote(e_send, e_land.at[n], e_sem, n, "inner", inner_at(rel, 1))
            for n, rel in enumerate(PEERS)
        ]
    )

    down = []
    for n, dz in enumerate(order):
        own = 2.0 * dot(low, piece(inner_at((0, dz), 1)), NN)
        cross[n].wait_recv()
        own = own + land_y[n].astype(jnp.float32)
        if dz:
            part_z[n] = own.astype(jnp.bfloat16)
            down.append(remote(part_z.at[n], land_z.at[n], pz_sem, n, "inner", inner_at((0, dz), 1)))
            down[-1].start()
    coulomb = own

    own_cols = jnp.transpose(own_xyz)
    for a in range(16):
        if a > 0:
            x_copies[a - 1].wait_recv()
        there = own_xyz if a == 0 else x_land[a - 1]
        r2 = jnp.zeros((128, 128), jnp.float32)
        for k in range(3):
            d = own_cols[:, k : k + 1] - there[k : k + 1, :]
            r2 = r2 + d * d
        hi, lo = split(lax.rsqrt(r2 + 1.0))
        k_hi[:, a * 128 : (a + 1) * 128] = hi
        k_lo[:, a * 128 : (a + 1) * 128] = lo

    for copy in e_copies:
        copy.wait_recv()
    total = e_row
    for n in range(N_IN):
        total = total + e_land[n]
    num = jnp.sum(jnp.where(lane16 == row16, total, 0.0), axis=1, keepdims=True)
    sq = jnp.sum(jnp.where(lane16 == row16 + 16, total, 0.0), axis=1, keepdims=True)
    energy = num / (sq + EPSILON)

    for n in reversed(range(N_Z)):
        down[n].wait_recv()
        coulomb = coulomb + land_z[n].astype(jnp.float32)

    sigma = gap * masked + active * coulomb
    refined = active * (masked - (sigma - energy * masked) / gap)
    refined_ref[...] = refined
    both = dot(refined.astype(jnp.bfloat16), chg_ref[...], NT)
    first = lane16[0:STATES] < 64
    own = jnp.where(first, both[0:STATES], both[STATES:])
    c_send[...] = own
    c_copies = start_all(
        [
            remote(c_send, c_land.at[n], c_sem, n, "inner", inner_at(rel, 1))
            for n, rel in enumerate(PEERS)
        ]
    )
    charges = own
    for n in reversed(range(N_IN)):
        c_copies[n].wait_recv()
        charges = charges + c_land[n]

    g_send[...] = charges
    g_copies = start_all(
        [remote(g_send, g_land.at[a - 1], g_sem, a - 1, "grp", grp_at(a, 1)) for a in range(1, 16)]
    )

    rows = jnp.concatenate([jnp.where(first, charges, 0.0), jnp.where(first, 0.0, charges)], axis=0)
    rows_hi, rows_lo = split(rows)
    with_hi = dot(jnp.concatenate([rows_hi, rows_lo], axis=0), k_hi[...], NN)
    field = with_hi[0:16] + with_hi[16:32] + dot(rows_hi, k_lo[...], NN)

    t = lax.rem(me, STATES)
    half = me // STATES
    in_half = (lax.broadcasted_iota(jnp.int32, (1, 128), 1) // 64) == half
    out_lane = lax.broadcasted_iota(jnp.int32, (16, 16), 1)
    out_row = lax.broadcasted_iota(jnp.int32, (16, 16), 0)
    for copies in ([to_y], to_z, onward, x_copies, cross, e_copies, down, c_copies):
        for c in copies:
            c.wait_send()
    block = jnp.zeros((16, 16), jnp.float32)
    for a in range(16):
        if a > 0:
            g_copies[a - 1].wait_recv()
        src = g_send if a == 0 else g_land.at[a - 1]
        q = jnp.where(in_half, src[pl.ds(t, 1), :], 0.0)
        column = jnp.sum(field[:, a * 128 : (a + 1) * 128] * q, axis=1, keepdims=True)
        block = jnp.where(out_lane == grp_at(a, -1), column, block)
    same = (out_lane == grp) & (out_row // STATES == half)
    block_ref[...] = jnp.where(same, jnp.where(out_row % STATES == t, energy, 0.0), block)
    for c in g_copies:
        c.wait_send()


def hand_over(refined_ref, block_ref, refined_hbm, block_hbm, rows, sems):
    big = pltpu.make_async_copy(refined_ref, refined_hbm, sems.at[0])
    big.start()
    for r in range(block_ref.shape[0]):
        rows[r] = block_ref[r : r + 1, :]
    small = pltpu.make_async_copy(rows, block_hbm, sems.at[1])
    small.start()
    big.wait()
    small.wait()


def local(
    amplitudes, factors, atom_charges, eps_occ, eps_vir, occ_count, vir_count, atom_list, positions
):
    monomers, states, pairs = amplitudes.shape
    aux, every = factors.shape[1:]
    rows = monomers * states
    vmem = pl.BlockSpec(memory_space=pltpu.VMEM)
    hbm = pl.BlockSpec(memory_space=pl.ANY)
    bf, f32, i32 = jnp.bfloat16, jnp.float32, jnp.int32
    by_tile = jnp.transpose(factors, (1, 0, 2)).reshape(aux, monomers, every // 128, 128)
    sem = pltpu.SemaphoreType.DMA
    refined, block = pl.pallas_call(
        kernel,
        name="exciton",
        out_shape=(
            pltpu.VMEM((rows, pairs), f32),
            pltpu.VMEM((rows, rows), f32),
        ),
        in_specs=[hbm] * 9,
        out_specs=(vmem, vmem),
        scratch_shapes=[
            pltpu.VMEM((rows, pairs), bf),
            pltpu.VMEM((monomers * 64, pairs), bf),
            pltpu.SMEM(eps_occ.shape, f32),
            pltpu.VMEM(eps_vir.shape, f32),
            pltpu.SMEM(occ_count.shape, i32),
            pltpu.SMEM(vir_count.shape, i32),
            pltpu.VMEM((1, 128), i32),
            pltpu.VMEM(positions.shape, f32),
            pltpu.VMEM((every // 128, 128, monomers, 128), bf),
            pltpu.VMEM((rows, pairs), bf),
            pltpu.VMEM((N_Z, rows, pairs), bf),
            pltpu.VMEM((N_Z, rows, pairs), bf),
            pltpu.VMEM((Z, rows, pairs), bf),
            pltpu.VMEM((Z, rows, pairs), bf),
            pltpu.VMEM((N_Z, rows, pairs), bf),
            pltpu.VMEM((N_Z, rows, pairs), bf),
            pltpu.VMEM((1, 128), f32),
            pltpu.VMEM((N_IN, 1, 128), f32),
            pltpu.VMEM((8, 128), f32),
            pltpu.VMEM((N_IN, 8, 128), f32),
            pltpu.VMEM((8, 128), f32),
            pltpu.VMEM((N_GRP, 8, 128), f32),
            pltpu.VMEM((8, 128), f32),
            pltpu.VMEM((N_GRP, 8, 128), f32),
            pltpu.VMEM((8, positions.shape[1]), f32),
            pltpu.VMEM((128, 2048), bf),
            pltpu.VMEM((128, 2048), bf),
            sem((8,)),
            sem,
            sem((2, 1)),
            sem((2, N_Z)),
            sem((2, N_Z)),
            sem((2, Z)),
            sem((2, N_Z)),
            sem((2, N_IN)),
            sem((2, N_IN)),
            sem((2, N_GRP)),
            sem((2, N_GRP)),
        ],
        compiler_params=pltpu.CompilerParams(collective_id=0, has_side_effects=True),
    )(
        amplitudes.reshape(rows, pairs),
        by_tile.transpose(0, 2, 1, 3),
        atom_charges.reshape(monomers * 64, pairs),
        eps_occ, eps_vir, occ_count, vir_count, atom_list.reshape(1, -1), positions,
    )
    refined, block = pl.pallas_call(
        hand_over,
        name="hand_over",
        out_shape=(
            jax.ShapeDtypeStruct((rows, pairs), f32),
            jax.ShapeDtypeStruct((rows, 1, rows), f32),
        ),
        in_specs=[vmem, vmem],
        out_specs=(hbm, hbm),
        scratch_shapes=[pltpu.VMEM((rows, 1, rows), f32), sem((2,))],
    )(*(pltpu.with_memory_space_constraint(a, pltpu.VMEM) for a in (refined, block)))
    return refined.reshape(monomers, states, pairs), jnp.swapaxes(block, 1, 2)


def solution(mesh):
    in_specs = (
        P("grp", None, "inner"),
        P("grp", "inner", None),
        P("grp", None, "inner"),
        P("grp", None),
        P("grp", None),
        P("grp"),
        P("grp"),
        P("grp"),
        P(),
    )
    out_specs = (P("grp", None, "inner"), P("grp", None, "inner"))
    return jax.shard_map(local, mesh=mesh, in_specs=in_specs, out_specs=out_specs, check_vma=False)
```

```python
import jax
import jax.numpy as jnp
from jax import lax
from jax.experimental import pallas as pl
from jax.experimental.pallas import tpu as pltpu
from jax.sharding import PartitionSpec as P

NVIR = 256
STATES = 8
EPSILON = 1e-06
Z = 8
MESH = pl.DeviceIdType.MESH
FAR_Z = (4, 3, 5, 2, 6, 1, 7)
STRAIGHT = (4, 3, 5)
SUMMED = (2, 6, 1, 7, 0)
PEERS = sorted(
    [(dy, dz) for dy in (0, 1) for dz in range(Z) if (dy, dz) != (0, 0)],
    key=lambda r: -(2 * r[0] + min(r[1], Z - r[1])),
)
N_IN = len(PEERS)
N_Z = len(FAR_Z)
CROWD = [(dy, a) for dy in (1, 0) for a in range(1, 16)]
N_GRP = 15
NT = (((1,), (1,)), ((), ()))
NN = (((1,), (0,)), ((), ()))


def split(x):
    high = x.astype(jnp.bfloat16)
    return high, (x - high.astype(jnp.float32)).astype(jnp.bfloat16)


def dot(a, b, dims):
    return lax.dot_general(a, b, dims, preferred_element_type=jnp.float32)


def inner_at(rel, sign):
    me = lax.axis_index("inner")
    y, z = me // Z, me % Z
    return lax.rem(y + rel[0], 2) * Z + lax.rem(z + sign * rel[1] + Z, Z)


def grp_at(step, sign):
    return lax.rem(lax.axis_index("grp") + sign * step + 16, 16)


def remote(src, dst, sems, n, axis, where):
    return remote_to(src, dst, sems, n, {axis: where})


def remote_to(src, dst, sems, n, device):
    return pltpu.make_async_remote_copy(
        src_ref=src,
        dst_ref=dst,
        send_sem=sems.at[0, n],
        recv_sem=sems.at[1, n],
        device_id=device,
        device_id_type=MESH,
    )


def start_all(copies):
    for c in copies:
        c.start()
    return copies


def kernel(
    amp_hbm, fac_hbm, chg_hbm, occ_e_hbm, vir_e_hbm, occ_n_hbm, vir_n_hbm, atoms_hbm, pos_hbm,
    refined_ref, block_ref,
    amp_ref, chg_ref, occ_e, vir_e, occ_n, vir_n, atoms_ref, pos_ref,
    fac, amp_y, amp_z, amp_yz, part_s, land_s, part_y, land_y, part_z, land_z,
    e_send, e_land, c_send, c_land, g_send, g_row, p_land, g_land, x_send, x_land, pos8, k_hi, k_lo,
    in_sem, fac_sem, ay_sem, az_sem, ayz_sem, ps_sem, py_sem, pz_sem, e_sem, c_sem, p_sem, g_sem, x_sem,
):
    me = lax.axis_index("inner")
    grp = lax.axis_index("grp")
    rows_n, pairs = amp_ref.shape
    segs = pairs // NVIR
    aux, tiles = fac_hbm.shape[:2]
    per = pairs // 128

    barrier = pltpu.get_barrier_semaphore()
    for rel in [(1, 0)] + [(0, dz) for dz in FAR_Z]:
        pl.semaphore_signal(barrier, inc=1, device_id={"inner": inner_at(rel, 1)}, device_id_type=MESH)
    for a in range(1, 16):
        pl.semaphore_signal(barrier, inc=1, device_id={"grp": grp_at(a, 1)}, device_id_type=MESH)
    pairs_in = [
        (amp_hbm, amp_ref), (vir_e_hbm, vir_e), (occ_e_hbm, occ_e), (occ_n_hbm, occ_n),
        (vir_n_hbm, vir_n), (atoms_hbm, atoms_ref), (pos_hbm, pos_ref), (chg_hbm, chg_ref),
    ]
    inputs = start_all(
        [pltpu.make_async_copy(src, dst, in_sem.at[n]) for n, (src, dst) in enumerate(pairs_in)]
    )
    loads = []
    for j in range(tiles):
        loads.append(pltpu.make_async_copy(fac_hbm.at[:, j], fac.at[j, pl.ds(0, aux)], fac_sem))
        loads[-1].start()
    for copy in inputs:
        copy.wait()

    pos8[...] = jnp.zeros_like(pos8)
    pos8[0:3, :] = pos_ref[...]
    p_all = pos8[...]
    p_hi = p_all.astype(jnp.bfloat16).astype(jnp.float32)
    p_mid = (p_all - p_hi).astype(jnp.bfloat16).astype(jnp.float32)
    p_lo = p_all - p_hi - p_mid
    hot = (
        (lax.broadcasted_iota(jnp.int32, (pos_ref.shape[1], 128), 0) == atoms_ref[...])
        .astype(jnp.float32)
        .astype(jnp.bfloat16)
    )
    xyz3 = dot(jnp.concatenate([p_hi, p_mid, p_lo], axis=0).astype(jnp.bfloat16), hot, NN)
    own_xyz = xyz3[0:8] + xyz3[8:16] + xyz3[16:24]
    x_send[...] = own_xyz

    lane = lax.broadcasted_iota(jnp.int32, (STATES, pairs), 1)
    seg, vir = lane // NVIR, lane % NVIR
    vir_in = [vir < vir_n[c] for c in range(2)]

    def active_of(who):
        return jnp.concatenate(
            [jnp.where(vir_in[c] & (seg + who * segs < occ_n[c]), 1.0, 0.0) for c in range(2)],
            axis=0,
        )

    active = active_of(me)
    gap = jnp.concatenate(
        [
            jnp.concatenate(
                [
                    jnp.broadcast_to(vir_e[c : c + 1, :] - occ_e[c, me * segs + m], (STATES, NVIR))
                    for m in range(segs)
                ],
                axis=1,
            )
            for c in range(2)
        ],
        axis=0,
    )
    masked = amp_ref[...].astype(jnp.float32) * active
    own_num = jnp.sum(gap * masked * masked, axis=1, keepdims=True)
    own_sq = jnp.sum(masked * masked, axis=1, keepdims=True)
    for j in range(tiles):
        fac[j, aux:128] = jnp.zeros((128 - aux, 2, 128), jnp.bfloat16)
    flat = fac.reshape(tiles, 256, 128)

    def piece(who):
        return jnp.concatenate([flat[who * per + m] for m in range(per)], axis=1)

    pl.semaphore_wait(barrier, 1 + N_Z + N_GRP)
    to_y = remote(amp_ref, amp_y, ay_sem, 0, "inner", inner_at((1, 0), 1))
    to_y.start()
    to_z = start_all(
        [
            remote(amp_ref, amp_z.at[n], az_sem, n, "inner", inner_at((0, dz), 1))
            for n, dz in enumerate(FAR_Z)
        ]
    )
    x_copies = start_all(
        [remote(x_send, x_land.at[a - 1], x_sem, a - 1, "grp", grp_at(a, 1)) for a in range(1, 16)]
    )
    for c in loads:
        c.wait()

    def fit(amps, who):
        theirs = (amps.astype(jnp.float32) * active_of(who)).astype(jnp.bfloat16)
        return dot(theirs, piece(who), NT)

    fitted = dot(masked.astype(jnp.bfloat16), piece(me), NT)
    onward = []
    for n in reversed(range(N_Z)):
        to_z[n].wait_recv()
        fitted = fitted + fit(amp_z[n], inner_at((0, FAR_Z[n]), -1))
        if n == N_Z - 2:
            to_y.wait_recv()
            onward = start_all(
                [
                    remote(amp_y, amp_yz.at[m], ayz_sem, m, "inner", inner_at((0, dz), 1))
                    for m, dz in enumerate(FAR_Z)
                ]
            )
            fitted = fitted + fit(amp_y[...], inner_at((1, 0), 1))
    for n in reversed(range(N_Z)):
        onward[n].wait_recv()
        fitted = fitted + fit(amp_yz[n], inner_at((1, FAR_Z[n]), -1))
    parity = lax.broadcasted_iota(jnp.int32, fitted.shape, 1) % 2
    monomer = lax.broadcasted_iota(jnp.int32, fitted.shape, 0) // STATES
    fitted = jnp.where(parity == monomer, fitted, 0.0)
    low = fitted.astype(jnp.bfloat16)

    def partial_to(rel):
        return 2.0 * dot(low, piece(inner_at(rel, 1)), NN)

    straight, cross, down = {}, {}, {}

    def send_straight(n):
        rel = (1, STRAIGHT[n])
        part_s[n] = partial_to(rel).astype(jnp.bfloat16)
        straight[n] = remote(part_s.at[n], land_s.at[n], ps_sem, n, "inner", inner_at(rel, 1))
        straight[n].start()

    def send_cross(n):
        part_y[n] = partial_to((1, SUMMED[n])).astype(jnp.bfloat16)
        cross[n] = remote(part_y.at[n], land_y.at[n], py_sem, n, "inner", inner_at((1, 0), 1))
        cross[n].start()

    def send_down(n, value):
        rel = (0, FAR_Z[n])
        part_z[n] = value.astype(jnp.bfloat16)
        down[n] = remote(part_z.at[n], land_z.at[n], pz_sem, n, "inner", inner_at(rel, 1))
        down[n].start()

    send_straight(0)
    send_cross(0)
    send_cross(1)

    row16 = lax.broadcasted_iota(jnp.int32, (rows_n, 128), 0)
    lane16 = lax.broadcasted_iota(jnp.int32, (rows_n, 128), 1)
    num = own_num + 2.0 * jnp.sum(low.astype(jnp.float32) * fitted, axis=1, keepdims=True)
    tile = jnp.where(lane16 == row16, num, 0.0) + jnp.where(lane16 == row16 + 16, own_sq, 0.0)
    e_row = jnp.sum(tile, axis=0, keepdims=True)
    e_send[...] = e_row
    e_copies = start_all(
        [
            remote(e_send, e_land.at[n], e_sem, n, "inner", inner_at(rel, 1))
            for n, rel in enumerate(PEERS)
        ]
    )
    send_straight(1)
    send_straight(2)
    send_cross(2)
    send_cross(3)
    for n in range(3):
        send_down(n, partial_to((0, FAR_Z[n])))
    send_cross(4)
    for n, dz in enumerate(SUMMED):
        own = partial_to((0, dz))
        cross[n].wait_recv()
        own = own + land_y[n].astype(jnp.float32)
        if dz:
            send_down(n + 3, own)
    coulomb = own

    own_cols = jnp.transpose(own_xyz)
    for a in range(16):
        if a > 0:
            x_copies[a - 1].wait_recv()
        there = own_xyz if a == 0 else x_land[a - 1]
        r2 = jnp.zeros((128, 128), jnp.float32)
        for k in range(3):
            d = own_cols[:, k : k + 1] - there[k : k + 1, :]
            r2 = r2 + d * d
        hi, lo = split(lax.rsqrt(r2 + 1.0))
        k_hi[:, a * 128 : (a + 1) * 128] = hi
        k_lo[:, a * 128 : (a + 1) * 128] = lo

    for copy in e_copies:
        copy.wait_recv()
    total = e_row
    for n in range(N_IN):
        total = total + e_land[n]
    num = jnp.sum(jnp.where(lane16 == row16, total, 0.0), axis=1, keepdims=True)
    sq = jnp.sum(jnp.where(lane16 == row16 + 16, total, 0.0), axis=1, keepdims=True)
    energy = num / (sq + EPSILON)

    for n in range(3):
        straight[n].wait_recv()
        coulomb = coulomb + land_s[n].astype(jnp.float32)
    for n in reversed(range(N_Z)):
        down[n].wait_recv()
        coulomb = coulomb + land_z[n].astype(jnp.float32)

    sigma = gap * masked + active * coulomb
    refined = active * (masked - (sigma - energy * masked) / gap)
    refined_ref[...] = refined
    both = dot(refined.astype(jnp.bfloat16), chg_ref[...], NT)
    first = lane16[0:STATES] < 64
    own = jnp.where(first, both[0:STATES], both[STATES:])
    c_send[...] = own
    c_copies = start_all(
        [
            remote(c_send, c_land.at[n], c_sem, n, "inner", inner_at((0, dz), 1))
            for n, dz in enumerate(FAR_Z)
        ]
    )
    charges = own
    for n in reversed(range(N_Z)):
        c_copies[n].wait_recv()
        charges = charges + c_land[n]
    g_send[...] = charges
    g_row[...] = g_send[pl.ds(lax.rem(me, STATES), 1), :]
    p_copy = remote(g_send, p_land, p_sem, 0, "inner", inner_at((1, 0), 1))
    p_copy.start()
    g_copies = start_all(
        [
            remote_to(
                g_row, g_land.at[n], g_sem, n,
                {"grp": grp_at(a, 1), "inner": inner_at((dy, 0), 1)},
            )
            for n, (dy, a) in enumerate(CROWD)
        ]
    )
    p_copy.wait_recv()
    p_row = p_land[pl.ds(lax.rem(me, STATES), 1), :]
    charges = charges + p_land[...]

    rows = jnp.concatenate([jnp.where(first, charges, 0.0), jnp.where(first, 0.0, charges)], axis=0)
    rows_hi, rows_lo = split(rows)
    with_hi = dot(jnp.concatenate([rows_hi, rows_lo], axis=0), k_hi[...], NN)
    field = with_hi[0:16] + with_hi[16:32] + dot(rows_hi, k_lo[...], NN)

    t = lax.rem(me, STATES)
    half = me // STATES
    in_half = (lax.broadcasted_iota(jnp.int32, (1, 128), 1) // 64) == half
    out_lane = lax.broadcasted_iota(jnp.int32, (16, 16), 1)
    out_row = lax.broadcasted_iota(jnp.int32, (16, 16), 0)
    for copies in ([to_y], to_z, onward, x_copies, straight.values(), cross.values(), e_copies, down.values(), c_copies):
        for c in copies:
            c.wait_send()
    p_copy.wait_send()
    block = jnp.zeros((16, 16), jnp.float32)
    for a in range(16):
        if a > 0:
            g_copies[a - 1].wait_recv()
            g_copies[a - 1 + N_GRP].wait_recv()
            q = g_land[a - 1] + g_land[a - 1 + N_GRP]
        else:
            q = g_row[...] + p_row
        q = jnp.where(in_half, q, 0.0)
        column = jnp.sum(field[:, a * 128 : (a + 1) * 128] * q, axis=1, keepdims=True)
        block = jnp.where(out_lane == grp_at(a, -1), column, block)
    same = (out_lane == grp) & (out_row // STATES == half)
    block_ref[...] = jnp.where(same, jnp.where(out_row % STATES == t, energy, 0.0), block)
    for c in g_copies:
        c.wait_send()


def hand_over(refined_ref, block_ref, refined_hbm, block_hbm, rows, sems):
    big = pltpu.make_async_copy(refined_ref, refined_hbm, sems.at[0])
    big.start()
    for r in range(block_ref.shape[0]):
        rows[r] = block_ref[r : r + 1, :]
    small = pltpu.make_async_copy(rows, block_hbm, sems.at[1])
    small.start()
    big.wait()
    small.wait()


def local(
    amplitudes, factors, atom_charges, eps_occ, eps_vir, occ_count, vir_count, atom_list, positions
):
    monomers, states, pairs = amplitudes.shape
    aux, every = factors.shape[1:]
    rows = monomers * states
    vmem = pl.BlockSpec(memory_space=pltpu.VMEM)
    hbm = pl.BlockSpec(memory_space=pl.ANY)
    bf, f32, i32 = jnp.bfloat16, jnp.float32, jnp.int32
    by_tile = jnp.transpose(factors, (1, 0, 2)).reshape(aux, monomers, every // 128, 128)
    sem = pltpu.SemaphoreType.DMA
    refined, block = pl.pallas_call(
        kernel,
        name="exciton",
        out_shape=(
            pltpu.VMEM((rows, pairs), f32),
            pltpu.VMEM((rows, rows), f32),
        ),
        in_specs=[hbm] * 9,
        out_specs=(vmem, vmem),
        scratch_shapes=[
            pltpu.VMEM((rows, pairs), bf),
            pltpu.VMEM((monomers * 64, pairs), bf),
            pltpu.SMEM(eps_occ.shape, f32),
            pltpu.VMEM(eps_vir.shape, f32),
            pltpu.SMEM(occ_count.shape, i32),
            pltpu.SMEM(vir_count.shape, i32),
            pltpu.VMEM((1, 128), i32),
            pltpu.VMEM(positions.shape, f32),
            pltpu.VMEM((every // 128, 128, monomers, 128), bf),
            pltpu.VMEM((rows, pairs), bf),
            pltpu.VMEM((N_Z, rows, pairs), bf),
            pltpu.VMEM((N_Z, rows, pairs), bf),
            pltpu.VMEM((3, rows, pairs), bf),
            pltpu.VMEM((3, rows, pairs), bf),
            pltpu.VMEM((5, rows, pairs), bf),
            pltpu.VMEM((5, rows, pairs), bf),
            pltpu.VMEM((N_Z, rows, pairs), bf),
            pltpu.VMEM((N_Z, rows, pairs), bf),
            pltpu.VMEM((1, 128), f32),
            pltpu.VMEM((N_IN, 1, 128), f32),
            pltpu.VMEM((8, 128), f32),
            pltpu.VMEM((N_Z, 8, 128), f32),
            pltpu.VMEM((8, 128), f32),
            pltpu.VMEM((1, 128), f32),
            pltpu.VMEM((8, 128), f32),
            pltpu.VMEM((2 * N_GRP, 1, 128), f32),
            pltpu.VMEM((8, 128), f32),
            pltpu.VMEM((N_GRP, 8, 128), f32),
            pltpu.VMEM((8, positions.shape[1]), f32),
            pltpu.VMEM((128, 2048), bf),
            pltpu.VMEM((128, 2048), bf),
            sem((8,)),
            sem,
            sem((2, 1)),
            sem((2, N_Z)),
            sem((2, N_Z)),
            sem((2, 3)),
            sem((2, 5)),
            sem((2, N_Z)),
            sem((2, N_IN)),
            sem((2, N_Z)),
            sem((2, 1)),
            sem((2, 2 * N_GRP)),
            sem((2, N_GRP)),
        ],
        compiler_params=pltpu.CompilerParams(collective_id=0, has_side_effects=True),
    )(
        amplitudes.reshape(rows, pairs),
        by_tile.transpose(0, 2, 1, 3),
        atom_charges.reshape(monomers * 64, pairs),
        eps_occ, eps_vir, occ_count, vir_count, atom_list.reshape(1, -1), positions,
    )
    refined, block = pl.pallas_call(
        hand_over,
        name="hand_over",
        out_shape=(
            jax.ShapeDtypeStruct((rows, pairs), f32),
            jax.ShapeDtypeStruct((rows, 1, rows), f32),
        ),
        in_specs=[vmem, vmem],
        out_specs=(hbm, hbm),
        scratch_shapes=[pltpu.VMEM((rows, 1, rows), f32), sem((2,))],
    )(*(pltpu.with_memory_space_constraint(a, pltpu.VMEM) for a in (refined, block)))
    return refined.reshape(monomers, states, pairs), jnp.swapaxes(block, 1, 2)


def solution(mesh):
    in_specs = (
        P("grp", None, "inner"),
        P("grp", "inner", None),
        P("grp", None, "inner"),
        P("grp", None),
        P("grp", None),
        P("grp"),
        P("grp"),
        P("grp"),
        P(),
    )
    out_specs = (P("grp", None, "inner"), P("grp", None, "inner"))
    return jax.shard_map(local, mesh=mesh, in_specs=in_specs, out_specs=out_specs, check_vma=False)
```

```python
import jax
import jax.numpy as jnp
from jax import lax
from jax.experimental import pallas as pl
from jax.experimental.pallas import tpu as pltpu
from jax.sharding import PartitionSpec as P

NVIR = 256
STATES = 8
EPSILON = 1e-06
Z = 8
MESH = pl.DeviceIdType.MESH
FAR_Z = (4, 3, 5, 2, 6, 1, 7)
NEAR_Z = (1, 7, 2, 6)
RELAYED = ((1, 2, 3), (7, 6, 5), (2, 2, 4))
ARRIVALS = (1, 7, 2, 6, 3, 5, 4)
PEERS = sorted(
    [(dy, dz) for dy in (0, 1) for dz in range(Z) if (dy, dz) != (0, 0)],
    key=lambda r: -(2 * r[0] + min(r[1], Z - r[1])),
)
N_IN = len(PEERS)
N_Z = len(FAR_Z)
CROWD = [(dy, a) for dy in (1, 0) for a in range(1, 16)]
N_GRP = 15
NT = (((1,), (1,)), ((), ()))
NN = (((1,), (0,)), ((), ()))


def split(x):
    high = x.astype(jnp.bfloat16)
    return high, (x - high.astype(jnp.float32)).astype(jnp.bfloat16)


def dot(a, b, dims):
    return lax.dot_general(a, b, dims, preferred_element_type=jnp.float32)


def inner_at(rel, sign):
    me = lax.axis_index("inner")
    y, z = me // Z, me % Z
    return lax.rem(y + rel[0], 2) * Z + lax.rem(z + sign * rel[1] + Z, Z)


def grp_at(step, sign):
    return lax.rem(lax.axis_index("grp") + sign * step + 16, 16)


def remote(src, dst, sems, n, axis, where):
    return remote_to(src, dst, sems, n, {axis: where})


def remote_to(src, dst, sems, n, device):
    return pltpu.make_async_remote_copy(
        src_ref=src,
        dst_ref=dst,
        send_sem=sems.at[0, n],
        recv_sem=sems.at[1, n],
        device_id=device,
        device_id_type=MESH,
    )


def start_all(copies):
    for c in copies:
        c.start()
    return copies


def kernel(
    amp_hbm, fac_hbm, chg_hbm, occ_e_hbm, vir_e_hbm, occ_n_hbm, vir_n_hbm, atoms_hbm, pos_hbm,
    refined_ref, block_ref,
    amp_ref, chg_ref, occ_e, vir_e, occ_n, vir_n, atoms_ref, pos_ref,
    fac, amp_z, amp_yz, part_y, land_y, part_z, land_z,
    e_send, e_land, c_send, c_land, g_send, g_row, p_land, g_land, x_send, x_land, pos8, k_hi, k_lo,
    in_sem, fac_sem, az_sem, ayz_sem, py_sem, pz_sem, e_sem, c_sem, p_sem, g_sem, x_sem,
):
    me = lax.axis_index("inner")
    grp = lax.axis_index("grp")
    rows_n, pairs = amp_ref.shape
    segs = pairs // NVIR
    aux, tiles = fac_hbm.shape[:2]
    per = pairs // 128

    barrier = pltpu.get_barrier_semaphore()
    for rel in [(1, 0)] + [(0, dz) for dz in NEAR_Z]:
        pl.semaphore_signal(barrier, inc=1, device_id={"inner": inner_at(rel, 1)}, device_id_type=MESH)
    for a in range(1, 16):
        pl.semaphore_signal(barrier, inc=1, device_id={"grp": grp_at(a, 1)}, device_id_type=MESH)
    pairs_in = [
        (amp_hbm, amp_ref), (vir_e_hbm, vir_e), (occ_e_hbm, occ_e), (occ_n_hbm, occ_n),
        (vir_n_hbm, vir_n), (atoms_hbm, atoms_ref), (pos_hbm, pos_ref), (chg_hbm, chg_ref),
    ]
    inputs = start_all(
        [pltpu.make_async_copy(src, dst, in_sem.at[n]) for n, (src, dst) in enumerate(pairs_in)]
    )
    inputs[0].wait()
    pl.semaphore_wait(barrier, 1 + len(NEAR_Z) + N_GRP)

    along, across = {}, {}

    def send_along(src, dz, at):
        n = ARRIVALS.index(at)
        along[at] = remote(src, amp_z.at[n], az_sem, n, "inner", inner_at((0, dz), 1))
        along[at].start()

    def send_across(src, at):
        n = ARRIVALS.index(at) + 1 if at else 0
        across[at] = remote(src, amp_yz.at[n], ayz_sem, n, "inner", inner_at((1, 0), 1))
        across[at].start()

    send_across(amp_ref, 0)
    for dz in NEAR_Z:
        send_along(amp_ref, dz, dz)
    loads = []
    for j in range(tiles):
        loads.append(pltpu.make_async_copy(fac_hbm.at[:, j], fac.at[j, pl.ds(0, aux)], fac_sem))
        loads[-1].start()
    for copy in inputs[1:]:
        copy.wait()

    pos8[...] = jnp.zeros_like(pos8)
    pos8[0:3, :] = pos_ref[...]
    p_all = pos8[...]
    p_hi = p_all.astype(jnp.bfloat16).astype(jnp.float32)
    p_mid = (p_all - p_hi).astype(jnp.bfloat16).astype(jnp.float32)
    p_lo = p_all - p_hi - p_mid
    hot = (
        (lax.broadcasted_iota(jnp.int32, (pos_ref.shape[1], 128), 0) == atoms_ref[...])
        .astype(jnp.float32)
        .astype(jnp.bfloat16)
    )
    xyz3 = dot(jnp.concatenate([p_hi, p_mid, p_lo], axis=0).astype(jnp.bfloat16), hot, NN)
    own_xyz = xyz3[0:8] + xyz3[8:16] + xyz3[16:24]
    x_send[...] = own_xyz

    for at, step, then in RELAYED:
        along[at].wait_recv()
        shard = amp_z.at[ARRIVALS.index(at)]
        send_along(shard, step, then)
        send_across(shard, at)
    along[6].wait_recv()
    send_across(amp_z.at[ARRIVALS.index(6)], 6)
    x_copies = start_all(
        [remote(x_send, x_land.at[a - 1], x_sem, a - 1, "grp", grp_at(a, 1)) for a in range(1, 16)]
    )
    lane = lax.broadcasted_iota(jnp.int32, (STATES, pairs), 1)
    seg, vir = lane // NVIR, lane % NVIR
    vir_in = [vir < vir_n[c] for c in range(2)]

    def active_of(who):
        return jnp.concatenate(
            [jnp.where(vir_in[c] & (seg + who * segs < occ_n[c]), 1.0, 0.0) for c in range(2)],
            axis=0,
        )

    active = active_of(me)
    gap = jnp.concatenate(
        [
            jnp.concatenate(
                [
                    jnp.broadcast_to(vir_e[c : c + 1, :] - occ_e[c, me * segs + m], (STATES, NVIR))
                    for m in range(segs)
                ],
                axis=1,
            )
            for c in range(2)
        ],
        axis=0,
    )
    masked = amp_ref[...].astype(jnp.float32) * active
    own_num = jnp.sum(gap * masked * masked, axis=1, keepdims=True)
    own_sq = jnp.sum(masked * masked, axis=1, keepdims=True)
    for j in range(tiles):
        fac[j, aux:128] = jnp.zeros((128 - aux, 2, 128), jnp.bfloat16)
    flat = fac.reshape(tiles, 256, 128)

    def piece(who):
        return jnp.concatenate([flat[who * per + m] for m in range(per)], axis=1)

    for c in loads:
        c.wait()

    def fit(amps, who):
        theirs = (amps.astype(jnp.float32) * active_of(who)).astype(jnp.bfloat16)
        return dot(theirs, piece(who), NT)

    def fit_along(at):
        return fit(amp_z[ARRIVALS.index(at)], inner_at((0, at), -1))

    def fit_across(at):
        across[at].wait_recv()
        return fit(amp_yz[ARRIVALS.index(at) + 1 if at else 0], inner_at((1, at), -1))

    fitted = dot(masked.astype(jnp.bfloat16), piece(me), NT) + fit_along(1) + fit_along(7)
    for at in (3, 5, 4):
        along[at].wait_recv()
        send_across(amp_z.at[ARRIVALS.index(at)], at)
    for at in (2, 6, 3, 5, 4):
        fitted = fitted + fit_along(at)
    for at in (0,) + ARRIVALS:
        fitted = fitted + fit_across(at)
    parity = lax.broadcasted_iota(jnp.int32, fitted.shape, 1) % 2
    monomer = lax.broadcasted_iota(jnp.int32, fitted.shape, 0) // STATES
    fitted = jnp.where(parity == monomer, fitted, 0.0)
    low = fitted.astype(jnp.bfloat16)

    order = FAR_Z + (0,)
    cross = []
    for n, dz in enumerate(order):
        part_y[n] = (2.0 * dot(low, piece(inner_at((1, dz), 1)), NN)).astype(jnp.bfloat16)
        cross.append(remote(part_y.at[n], land_y.at[n], py_sem, n, "inner", inner_at((1, 0), 1)))
        cross[-1].start()

    row16 = lax.broadcasted_iota(jnp.int32, (rows_n, 128), 0)
    lane16 = lax.broadcasted_iota(jnp.int32, (rows_n, 128), 1)
    num = own_num + 2.0 * jnp.sum(low.astype(jnp.float32) * fitted, axis=1, keepdims=True)
    tile = jnp.where(lane16 == row16, num, 0.0) + jnp.where(lane16 == row16 + 16, own_sq, 0.0)
    e_row = jnp.sum(tile, axis=0, keepdims=True)
    e_send[...] = e_row
    e_copies = start_all(
        [
            remote(e_send, e_land.at[n], e_sem, n, "inner", inner_at(rel, 1))
            for n, rel in enumerate(PEERS)
        ]
    )

    down = []
    for n, dz in enumerate(order):
        own = 2.0 * dot(low, piece(inner_at((0, dz), 1)), NN)
        cross[n].wait_recv()
        own = own + land_y[n].astype(jnp.float32)
        if dz:
            part_z[n] = own.astype(jnp.bfloat16)
            down.append(remote(part_z.at[n], land_z.at[n], pz_sem, n, "inner", inner_at((0, dz), 1)))
            down[-1].start()
    coulomb = own

    own_cols = jnp.transpose(own_xyz)
    for a in range(16):
        if a > 0:
            x_copies[a - 1].wait_recv()
        there = own_xyz if a == 0 else x_land[a - 1]
        r2 = jnp.zeros((128, 128), jnp.float32)
        for k in range(3):
            d = own_cols[:, k : k + 1] - there[k : k + 1, :]
            r2 = r2 + d * d
        hi, lo = split(lax.rsqrt(r2 + 1.0))
        k_hi[:, a * 128 : (a + 1) * 128] = hi
        k_lo[:, a * 128 : (a + 1) * 128] = lo

    for copy in e_copies:
        copy.wait_recv()
    total = e_row
    for n in range(N_IN):
        total = total + e_land[n]
    num = jnp.sum(jnp.where(lane16 == row16, total, 0.0), axis=1, keepdims=True)
    sq = jnp.sum(jnp.where(lane16 == row16 + 16, total, 0.0), axis=1, keepdims=True)
    energy = num / (sq + EPSILON)

    for n in reversed(range(N_Z)):
        down[n].wait_recv()
        coulomb = coulomb + land_z[n].astype(jnp.float32)

    sigma = gap * masked + active * coulomb
    refined = active * (masked - (sigma - energy * masked) / gap)
    refined_ref[...] = refined
    both = dot(refined.astype(jnp.bfloat16), chg_ref[...], NT)
    first = lane16[0:STATES] < 64
    own = jnp.where(first, both[0:STATES], both[STATES:])
    c_send[...] = own
    c_copies = start_all(
        [
            remote(c_send, c_land.at[n], c_sem, n, "inner", inner_at((0, dz), 1))
            for n, dz in enumerate(FAR_Z)
        ]
    )
    charges = own
    for n in reversed(range(N_Z)):
        c_copies[n].wait_recv()
        charges = charges + c_land[n]
    g_send[...] = charges
    g_row[...] = g_send[pl.ds(lax.rem(me, STATES), 1), :]
    p_copy = remote(g_send, p_land, p_sem, 0, "inner", inner_at((1, 0), 1))
    p_copy.start()
    g_copies = start_all(
        [
            remote_to(
                g_row, g_land.at[n], g_sem, n,
                {"grp": grp_at(a, 1), "inner": inner_at((dy, 0), 1)},
            )
            for n, (dy, a) in enumerate(CROWD)
        ]
    )
    p_copy.wait_recv()
    p_row = p_land[pl.ds(lax.rem(me, STATES), 1), :]
    charges = charges + p_land[...]

    rows = jnp.concatenate([jnp.where(first, charges, 0.0), jnp.where(first, 0.0, charges)], axis=0)
    rows_hi, rows_lo = split(rows)
    with_hi = dot(jnp.concatenate([rows_hi, rows_lo], axis=0), k_hi[...], NN)
    field = with_hi[0:16] + with_hi[16:32] + dot(rows_hi, k_lo[...], NN)

    t = lax.rem(me, STATES)
    half = me // STATES
    in_half = (lax.broadcasted_iota(jnp.int32, (1, 128), 1) // 64) == half
    out_lane = lax.broadcasted_iota(jnp.int32, (16, 16), 1)
    out_row = lax.broadcasted_iota(jnp.int32, (16, 16), 0)
    for copies in (along.values(), across.values(), x_copies, cross, e_copies, down, c_copies):
        for c in copies:
            c.wait_send()
    p_copy.wait_send()
    block = jnp.zeros((16, 16), jnp.float32)
    for a in range(16):
        if a > 0:
            g_copies[a - 1].wait_recv()
            g_copies[a - 1 + N_GRP].wait_recv()
            q = g_land[a - 1] + g_land[a - 1 + N_GRP]
        else:
            q = g_row[...] + p_row
        q = jnp.where(in_half, q, 0.0)
        column = jnp.sum(field[:, a * 128 : (a + 1) * 128] * q, axis=1, keepdims=True)
        block = jnp.where(out_lane == grp_at(a, -1), column, block)
    same = (out_lane == grp) & (out_row // STATES == half)
    block_ref[...] = jnp.where(same, jnp.where(out_row % STATES == t, energy, 0.0), block)
    for c in g_copies:
        c.wait_send()


def hand_over(refined_ref, block_ref, refined_hbm, block_hbm, rows, sems):
    big = pltpu.make_async_copy(refined_ref, refined_hbm, sems.at[0])
    big.start()
    for r in range(block_ref.shape[0]):
        rows[r] = block_ref[r : r + 1, :]
    small = pltpu.make_async_copy(rows, block_hbm, sems.at[1])
    small.start()
    big.wait()
    small.wait()


def local(
    amplitudes, factors, atom_charges, eps_occ, eps_vir, occ_count, vir_count, atom_list, positions
):
    monomers, states, pairs = amplitudes.shape
    aux, every = factors.shape[1:]
    rows = monomers * states
    vmem = pl.BlockSpec(memory_space=pltpu.VMEM)
    hbm = pl.BlockSpec(memory_space=pl.ANY)
    bf, f32, i32 = jnp.bfloat16, jnp.float32, jnp.int32
    by_tile = jnp.transpose(factors, (1, 0, 2)).reshape(aux, monomers, every // 128, 128)
    sem = pltpu.SemaphoreType.DMA
    refined, block = pl.pallas_call(
        kernel,
        name="exciton",
        out_shape=(
            pltpu.VMEM((rows, pairs), f32),
            pltpu.VMEM((rows, rows), f32),
        ),
        in_specs=[hbm] * 9,
        out_specs=(vmem, vmem),
        scratch_shapes=[
            pltpu.VMEM((rows, pairs), bf),
            pltpu.VMEM((monomers * 64, pairs), bf),
            pltpu.SMEM(eps_occ.shape, f32),
            pltpu.VMEM(eps_vir.shape, f32),
            pltpu.SMEM(occ_count.shape, i32),
            pltpu.SMEM(vir_count.shape, i32),
            pltpu.VMEM((1, 128), i32),
            pltpu.VMEM(positions.shape, f32),
            pltpu.VMEM((every // 128, 128, monomers, 128), bf),
            pltpu.VMEM((N_Z, rows, pairs), bf),
            pltpu.VMEM((Z, rows, pairs), bf),
            pltpu.VMEM((Z, rows, pairs), bf),
            pltpu.VMEM((Z, rows, pairs), bf),
            pltpu.VMEM((N_Z, rows, pairs), bf),
            pltpu.VMEM((N_Z, rows, pairs), bf),
            pltpu.VMEM((1, 128), f32),
            pltpu.VMEM((N_IN, 1, 128), f32),
            pltpu.VMEM((8, 128), f32),
            pltpu.VMEM((N_Z, 8, 128), f32),
            pltpu.VMEM((8, 128), f32),
            pltpu.VMEM((1, 128), f32),
            pltpu.VMEM((8, 128), f32),
            pltpu.VMEM((2 * N_GRP, 1, 128), f32),
            pltpu.VMEM((8, 128), f32),
            pltpu.VMEM((N_GRP, 8, 128), f32),
            pltpu.VMEM((8, positions.shape[1]), f32),
            pltpu.VMEM((128, 2048), bf),
            pltpu.VMEM((128, 2048), bf),
            sem((8,)),
            sem,
            sem((2, N_Z)),
            sem((2, Z)),
            sem((2, Z)),
            sem((2, N_Z)),
            sem((2, N_IN)),
            sem((2, N_Z)),
            sem((2, 1)),
            sem((2, 2 * N_GRP)),
            sem((2, N_GRP)),
        ],
        compiler_params=pltpu.CompilerParams(collective_id=0, has_side_effects=True),
    )(
        amplitudes.reshape(rows, pairs),
        by_tile.transpose(0, 2, 1, 3),
        atom_charges.reshape(monomers * 64, pairs),
        eps_occ, eps_vir, occ_count, vir_count, atom_list.reshape(1, -1), positions,
    )
    refined, block = pl.pallas_call(
        hand_over,
        name="hand_over",
        out_shape=(
            jax.ShapeDtypeStruct((rows, pairs), f32),
            jax.ShapeDtypeStruct((rows, 1, rows), f32),
        ),
        in_specs=[vmem, vmem],
        out_specs=(hbm, hbm),
        scratch_shapes=[pltpu.VMEM((rows, 1, rows), f32), sem((2,))],
    )(*(pltpu.with_memory_space_constraint(a, pltpu.VMEM) for a in (refined, block)))
    return refined.reshape(monomers, states, pairs), jnp.swapaxes(block, 1, 2)


def solution(mesh):
    in_specs = (
        P("grp", None, "inner"),
        P("grp", "inner", None),
        P("grp", None, "inner"),
        P("grp", None),
        P("grp", None),
        P("grp"),
        P("grp"),
        P("grp"),
        P(),
    )
    out_specs = (P("grp", None, "inner"), P("grp", None, "inner"))
    return jax.shard_map(local, mesh=mesh, in_specs=in_specs, out_specs=out_specs, check_vma=False)
```

```python
import jax
import jax.numpy as jnp
from jax import lax
from jax.experimental import pallas as pl
from jax.experimental.pallas import tpu as pltpu
from jax.sharding import PartitionSpec as P

NVIR = 256
STATES = 8
EPSILON = 1e-06
Z = 8
MESH = pl.DeviceIdType.MESH
FAR_Z = (4, 3, 5, 2, 6, 1, 7)
ARRIVALS = (1, 7, 2, 6, 3, 5, 4)
PEERS = sorted(
    [(dy, dz) for dy in (0, 1) for dz in range(Z) if (dy, dz) != (0, 0)],
    key=lambda r: -(2 * r[0] + min(r[1], Z - r[1])),
)
N_IN = len(PEERS)
N_Z = len(FAR_Z)
CROWD = [(dy, a) for dy in (1, 0) for a in range(1, 16)]
N_GRP = 15
NT = (((1,), (1,)), ((), ()))
NN = (((1,), (0,)), ((), ()))


def split(x):
    high = x.astype(jnp.bfloat16)
    return high, (x - high.astype(jnp.float32)).astype(jnp.bfloat16)


def dot(a, b, dims):
    return lax.dot_general(a, b, dims, preferred_element_type=jnp.float32)


def inner_at(rel, sign):
    me = lax.axis_index("inner")
    y, z = me // Z, me % Z
    return lax.rem(y + rel[0], 2) * Z + lax.rem(z + sign * rel[1] + Z, Z)


def grp_at(step, sign):
    return lax.rem(lax.axis_index("grp") + sign * step + 16, 16)


def remote(src, dst, sems, n, axis, where):
    return remote_to(src, dst, sems, n, {axis: where})


def remote_to(src, dst, sems, n, device):
    return pltpu.make_async_remote_copy(
        src_ref=src,
        dst_ref=dst,
        send_sem=sems.at[0, n],
        recv_sem=sems.at[1, n],
        device_id=device,
        device_id_type=MESH,
    )


def start_all(copies):
    for c in copies:
        c.start()
    return copies


def kernel(
    amp_hbm, fac_hbm, chg_hbm, occ_e_hbm, vir_e_hbm, occ_n_hbm, vir_n_hbm, atoms_hbm, pos_hbm,
    refined_ref, block_ref,
    amp_ref, chg_ref, occ_e, vir_e, occ_n, vir_n, atoms_ref, pos_ref,
    fac, amp_z, amp_yz, part_y, land_y, part_z, land_z,
    e_send, e_land, c_send, c_land, g_send, g_row, p_land, g_land, x_send, x_land, pos8, k_hi, k_lo,
    in_sem, fac_sem, az_sem, ayz_sem, py_sem, pz_sem, e_sem, c_sem, p_sem, g_sem, x_sem,
):
    me = lax.axis_index("inner")
    grp = lax.axis_index("grp")
    rows_n, pairs = amp_ref.shape
    segs = pairs // NVIR
    aux, tiles = fac_hbm.shape[:2]
    per = pairs // 128

    barrier = pltpu.get_barrier_semaphore()
    for rel in [(1, 0)] + [(0, dz) for dz in FAR_Z]:
        pl.semaphore_signal(barrier, inc=1, device_id={"inner": inner_at(rel, 1)}, device_id_type=MESH)
    for a in range(1, 16):
        pl.semaphore_signal(barrier, inc=1, device_id={"grp": grp_at(a, 1)}, device_id_type=MESH)
    pairs_in = [
        (amp_hbm, amp_ref), (vir_e_hbm, vir_e), (occ_e_hbm, occ_e), (occ_n_hbm, occ_n),
        (vir_n_hbm, vir_n), (atoms_hbm, atoms_ref), (pos_hbm, pos_ref), (chg_hbm, chg_ref),
    ]
    inputs = start_all(
        [pltpu.make_async_copy(src, dst, in_sem.at[n]) for n, (src, dst) in enumerate(pairs_in)]
    )
    inputs[0].wait()
    pl.semaphore_wait(barrier, 1 + len(FAR_Z) + N_GRP)

    along, across = {}, {}

    def send_along(src, dz, at):
        n = ARRIVALS.index(at)
        along[at] = remote(src, amp_z.at[n], az_sem, n, "inner", inner_at((0, dz), 1))
        along[at].start()

    def send_across(src, at):
        n = ARRIVALS.index(at) + 1 if at else 0
        across[at] = remote(src, amp_yz.at[n], ayz_sem, n, "inner", inner_at((1, 0), 1))
        across[at].start()

    send_across(amp_ref, 0)
    for dz in FAR_Z:
        send_along(amp_ref, dz, dz)
    loads = []
    for j in range(tiles):
        loads.append(pltpu.make_async_copy(fac_hbm.at[:, j], fac.at[j, pl.ds(0, aux)], fac_sem))
        loads[-1].start()
    for copy in inputs[1:]:
        copy.wait()

    pos8[...] = jnp.zeros_like(pos8)
    pos8[0:3, :] = pos_ref[...]
    p_all = pos8[...]
    p_hi = p_all.astype(jnp.bfloat16).astype(jnp.float32)
    p_mid = (p_all - p_hi).astype(jnp.bfloat16).astype(jnp.float32)
    p_lo = p_all - p_hi - p_mid
    hot = (
        (lax.broadcasted_iota(jnp.int32, (pos_ref.shape[1], 128), 0) == atoms_ref[...])
        .astype(jnp.float32)
        .astype(jnp.bfloat16)
    )
    xyz3 = dot(jnp.concatenate([p_hi, p_mid, p_lo], axis=0).astype(jnp.bfloat16), hot, NN)
    own_xyz = xyz3[0:8] + xyz3[8:16] + xyz3[16:24]
    x_send[...] = own_xyz

    for at in (1, 7, 2, 6):
        along[at].wait_recv()
        send_across(amp_z.at[ARRIVALS.index(at)], at)
    x_copies = start_all(
        [remote(x_send, x_land.at[a - 1], x_sem, a - 1, "grp", grp_at(a, 1)) for a in range(1, 16)]
    )
    lane = lax.broadcasted_iota(jnp.int32, (STATES, pairs), 1)
    seg, vir = lane // NVIR, lane % NVIR
    vir_in = [vir < vir_n[c] for c in range(2)]

    def active_of(who):
        return jnp.concatenate(
            [jnp.where(vir_in[c] & (seg + who * segs < occ_n[c]), 1.0, 0.0) for c in range(2)],
            axis=0,
        )

    active = active_of(me)
    gap = jnp.concatenate(
        [
            jnp.concatenate(
                [
                    jnp.broadcast_to(vir_e[c : c + 1, :] - occ_e[c, me * segs + m], (STATES, NVIR))
                    for m in range(segs)
                ],
                axis=1,
            )
            for c in range(2)
        ],
        axis=0,
    )
    masked = amp_ref[...].astype(jnp.float32) * active
    own_num = jnp.sum(gap * masked * masked, axis=1, keepdims=True)
    own_sq = jnp.sum(masked * masked, axis=1, keepdims=True)
    for j in range(tiles):
        fac[j, aux:128] = jnp.zeros((128 - aux, 2, 128), jnp.bfloat16)
    flat = fac.reshape(tiles, 256, 128)

    def piece(who):
        return jnp.concatenate([flat[who * per + m] for m in range(per)], axis=1)

    for c in loads:
        c.wait()

    def fit(amps, who):
        theirs = (amps.astype(jnp.float32) * active_of(who)).astype(jnp.bfloat16)
        return dot(theirs, piece(who), NT)

    def fit_along(at):
        return fit(amp_z[ARRIVALS.index(at)], inner_at((0, at), -1))

    def fit_across(at):
        across[at].wait_recv()
        return fit(amp_yz[ARRIVALS.index(at) + 1 if at else 0], inner_at((1, at), -1))

    fitted = dot(masked.astype(jnp.bfloat16), piece(me), NT) + fit_along(1) + fit_along(7)
    for at in (3, 5, 4):
        along[at].wait_recv()
        send_across(amp_z.at[ARRIVALS.index(at)], at)
    for at in (2, 6, 3, 5, 4):
        fitted = fitted + fit_along(at)
    for at in (0,) + ARRIVALS:
        fitted = fitted + fit_across(at)
    parity = lax.broadcasted_iota(jnp.int32, fitted.shape, 1) % 2
    monomer = lax.broadcasted_iota(jnp.int32, fitted.shape, 0) // STATES
    fitted = jnp.where(parity == monomer, fitted, 0.0)
    low = fitted.astype(jnp.bfloat16)

    order = FAR_Z + (0,)
    cross = []
    for n, dz in enumerate(order):
        part_y[n] = (2.0 * dot(low, piece(inner_at((1, dz), 1)), NN)).astype(jnp.bfloat16)
        cross.append(remote(part_y.at[n], land_y.at[n], py_sem, n, "inner", inner_at((1, 0), 1)))
        cross[-1].start()

    row16 = lax.broadcasted_iota(jnp.int32, (rows_n, 128), 0)
    lane16 = lax.broadcasted_iota(jnp.int32, (rows_n, 128), 1)
    num = own_num + 2.0 * jnp.sum(low.astype(jnp.float32) * fitted, axis=1, keepdims=True)
    tile = jnp.where(lane16 == row16, num, 0.0) + jnp.where(lane16 == row16 + 16, own_sq, 0.0)
    e_row = jnp.sum(tile, axis=0, keepdims=True)
    e_send[...] = e_row
    e_copies = start_all(
        [
            remote(e_send, e_land.at[n], e_sem, n, "inner", inner_at(rel, 1))
            for n, rel in enumerate(PEERS)
        ]
    )

    down = []
    for n, dz in enumerate(order):
        own = 2.0 * dot(low, piece(inner_at((0, dz), 1)), NN)
        cross[n].wait_recv()
        own = own + land_y[n].astype(jnp.float32)
        if dz:
            part_z[n] = own.astype(jnp.bfloat16)
            down.append(remote(part_z.at[n], land_z.at[n], pz_sem, n, "inner", inner_at((0, dz), 1)))
            down[-1].start()
    coulomb = own

    own_cols = jnp.transpose(own_xyz)
    for a in range(16):
        if a > 0:
            x_copies[a - 1].wait_recv()
        there = own_xyz if a == 0 else x_land[a - 1]
        r2 = jnp.zeros((128, 128), jnp.float32)
        for k in range(3):
            d = own_cols[:, k : k + 1] - there[k : k + 1, :]
            r2 = r2 + d * d
        hi, lo = split(lax.rsqrt(r2 + 1.0))
        k_hi[:, a * 128 : (a + 1) * 128] = hi
        k_lo[:, a * 128 : (a + 1) * 128] = lo

    for copy in e_copies:
        copy.wait_recv()
    total = e_row
    for n in range(N_IN):
        total = total + e_land[n]
    num = jnp.sum(jnp.where(lane16 == row16, total, 0.0), axis=1, keepdims=True)
    sq = jnp.sum(jnp.where(lane16 == row16 + 16, total, 0.0), axis=1, keepdims=True)
    energy = num / (sq + EPSILON)

    for n in reversed(range(N_Z)):
        down[n].wait_recv()
        coulomb = coulomb + land_z[n].astype(jnp.float32)

    sigma = gap * masked + active * coulomb
    refined = active * (masked - (sigma - energy * masked) / gap)
    refined_ref[...] = refined
    both = dot(refined.astype(jnp.bfloat16), chg_ref[...], NT)
    first = lane16[0:STATES] < 64
    own = jnp.where(first, both[0:STATES], both[STATES:])
    c_send[...] = own
    c_copies = start_all(
        [
            remote(c_send, c_land.at[n], c_sem, n, "inner", inner_at((0, dz), 1))
            for n, dz in enumerate(FAR_Z)
        ]
    )
    charges = own
    for n in reversed(range(N_Z)):
        c_copies[n].wait_recv()
        charges = charges + c_land[n]
    g_send[...] = charges
    g_row[...] = g_send[pl.ds(lax.rem(me, STATES), 1), :]
    p_copy = remote(g_send, p_land, p_sem, 0, "inner", inner_at((1, 0), 1))
    p_copy.start()
    g_copies = start_all(
        [
            remote_to(
                g_row, g_land.at[n], g_sem, n,
                {"grp": grp_at(a, 1), "inner": inner_at((dy, 0), 1)},
            )
            for n, (dy, a) in enumerate(CROWD)
        ]
    )
    p_copy.wait_recv()
    p_row = p_land[pl.ds(lax.rem(me, STATES), 1), :]
    charges = charges + p_land[...]

    rows = jnp.concatenate([jnp.where(first, charges, 0.0), jnp.where(first, 0.0, charges)], axis=0)
    rows_hi, rows_lo = split(rows)
    with_hi = dot(jnp.concatenate([rows_hi, rows_lo], axis=0), k_hi[...], NN)
    field = with_hi[0:16] + with_hi[16:32] + dot(rows_hi, k_lo[...], NN)

    t = lax.rem(me, STATES)
    half = me // STATES
    in_half = (lax.broadcasted_iota(jnp.int32, (1, 128), 1) // 64) == half
    out_lane = lax.broadcasted_iota(jnp.int32, (16, 16), 1)
    out_row = lax.broadcasted_iota(jnp.int32, (16, 16), 0)
    for copies in (along.values(), across.values(), x_copies, cross, e_copies, down, c_copies):
        for c in copies:
            c.wait_send()
    p_copy.wait_send()
    block = jnp.zeros((16, 16), jnp.float32)
    for a in range(16):
        if a > 0:
            g_copies[a - 1].wait_recv()
            g_copies[a - 1 + N_GRP].wait_recv()
            q = g_land[a - 1] + g_land[a - 1 + N_GRP]
        else:
            q = g_row[...] + p_row
        q = jnp.where(in_half, q, 0.0)
        column = jnp.sum(field[:, a * 128 : (a + 1) * 128] * q, axis=1, keepdims=True)
        block = jnp.where(out_lane == grp_at(a, -1), column, block)
    same = (out_lane == grp) & (out_row // STATES == half)
    block_ref[...] = jnp.where(same, jnp.where(out_row % STATES == t, energy, 0.0), block)
    for c in g_copies:
        c.wait_send()


def hand_over(refined_ref, block_ref, refined_hbm, block_hbm, rows, sems):
    big = pltpu.make_async_copy(refined_ref, refined_hbm, sems.at[0])
    big.start()
    for r in range(block_ref.shape[0]):
        rows[r] = block_ref[r : r + 1, :]
    small = pltpu.make_async_copy(rows, block_hbm, sems.at[1])
    small.start()
    big.wait()
    small.wait()


def local(
    amplitudes, factors, atom_charges, eps_occ, eps_vir, occ_count, vir_count, atom_list, positions
):
    monomers, states, pairs = amplitudes.shape
    aux, every = factors.shape[1:]
    rows = monomers * states
    vmem = pl.BlockSpec(memory_space=pltpu.VMEM)
    hbm = pl.BlockSpec(memory_space=pl.ANY)
    bf, f32, i32 = jnp.bfloat16, jnp.float32, jnp.int32
    by_tile = jnp.transpose(factors, (1, 0, 2)).reshape(aux, monomers, every // 128, 128)
    sem = pltpu.SemaphoreType.DMA
    refined, block = pl.pallas_call(
        kernel,
        name="exciton",
        out_shape=(
            pltpu.VMEM((rows, pairs), f32),
            pltpu.VMEM((rows, rows), f32),
        ),
        in_specs=[hbm] * 9,
        out_specs=(vmem, vmem),
        scratch_shapes=[
            pltpu.VMEM((rows, pairs), bf),
            pltpu.VMEM((monomers * 64, pairs), bf),
            pltpu.SMEM(eps_occ.shape, f32),
            pltpu.VMEM(eps_vir.shape, f32),
            pltpu.SMEM(occ_count.shape, i32),
            pltpu.SMEM(vir_count.shape, i32),
            pltpu.VMEM((1, 128), i32),
            pltpu.VMEM(positions.shape, f32),
            pltpu.VMEM((every // 128, 128, monomers, 128), bf),
            pltpu.VMEM((N_Z, rows, pairs), bf),
            pltpu.VMEM((Z, rows, pairs), bf),
            pltpu.VMEM((Z, rows, pairs), bf),
            pltpu.VMEM((Z, rows, pairs), bf),
            pltpu.VMEM((N_Z, rows, pairs), bf),
            pltpu.VMEM((N_Z, rows, pairs), bf),
            pltpu.VMEM((1, 128), f32),
            pltpu.VMEM((N_IN, 1, 128), f32),
            pltpu.VMEM((8, 128), f32),
            pltpu.VMEM((N_Z, 8, 128), f32),
            pltpu.VMEM((8, 128), f32),
            pltpu.VMEM((1, 128), f32),
            pltpu.VMEM((8, 128), f32),
            pltpu.VMEM((2 * N_GRP, 1, 128), f32),
            pltpu.VMEM((8, 128), f32),
            pltpu.VMEM((N_GRP, 8, 128), f32),
            pltpu.VMEM((8, positions.shape[1]), f32),
            pltpu.VMEM((128, 2048), bf),
            pltpu.VMEM((128, 2048), bf),
            sem((8,)),
            sem,
            sem((2, N_Z)),
            sem((2, Z)),
            sem((2, Z)),
            sem((2, N_Z)),
            sem((2, N_IN)),
            sem((2, N_Z)),
            sem((2, 1)),
            sem((2, 2 * N_GRP)),
            sem((2, N_GRP)),
        ],
        compiler_params=pltpu.CompilerParams(collective_id=0, has_side_effects=True),
    )(
        amplitudes.reshape(rows, pairs),
        by_tile.transpose(0, 2, 1, 3),
        atom_charges.reshape(monomers * 64, pairs),
        eps_occ, eps_vir, occ_count, vir_count, atom_list.reshape(1, -1), positions,
    )
    refined, block = pl.pallas_call(
        hand_over,
        name="hand_over",
        out_shape=(
            jax.ShapeDtypeStruct((rows, pairs), f32),
            jax.ShapeDtypeStruct((rows, 1, rows), f32),
        ),
        in_specs=[vmem, vmem],
        out_specs=(hbm, hbm),
        scratch_shapes=[pltpu.VMEM((rows, 1, rows), f32), sem((2,))],
    )(*(pltpu.with_memory_space_constraint(a, pltpu.VMEM) for a in (refined, block)))
    return refined.reshape(monomers, states, pairs), jnp.swapaxes(block, 1, 2)


def solution(mesh):
    in_specs = (
        P("grp", None, "inner"),
        P("grp", "inner", None),
        P("grp", None, "inner"),
        P("grp", None),
        P("grp", None),
        P("grp"),
        P("grp"),
        P("grp"),
        P(),
    )
    out_specs = (P("grp", None, "inner"), P("grp", None, "inner"))
    return jax.shard_map(local, mesh=mesh, in_specs=in_specs, out_specs=out_specs, check_vma=False)
```

```python
import jax
import jax.numpy as jnp
from jax import lax
from jax.experimental import pallas as pl
from jax.experimental.pallas import tpu as pltpu
from jax.sharding import PartitionSpec as P

NVIR = 256
STATES = 8
EPSILON = 1e-06
Z = 8
MESH = pl.DeviceIdType.MESH
FAR_Z = (4, 3, 5, 2, 6, 1, 7)
NEAR_Z = (1, 7, 2, 6)
RELAYED = ((1, 2, 3), (7, 6, 5), (2, 2, 4))
ARRIVALS = (1, 7, 2, 6, 3, 5, 4)
ORDER = [(dy, dz) for dy in (0, 1) for dz in (0,) + ARRIVALS]
GROUP = 4
PEERS = sorted(
    [(dy, dz) for dy in (0, 1) for dz in range(Z) if (dy, dz) != (0, 0)],
    key=lambda r: -(2 * r[0] + min(r[1], Z - r[1])),
)
N_IN = len(PEERS)
N_Z = len(FAR_Z)
CROWD = [(dy, a) for dy in (1, 0) for a in range(1, 16)]
N_GRP = 15
NT = (((1,), (1,)), ((), ()))
NN = (((1,), (0,)), ((), ()))


def split(x):
    high = x.astype(jnp.bfloat16)
    return high, (x - high.astype(jnp.float32)).astype(jnp.bfloat16)


def dot(a, b, dims):
    return lax.dot_general(a, b, dims, preferred_element_type=jnp.float32)


def inner_at(rel, sign):
    me = lax.axis_index("inner")
    y, z = me // Z, me % Z
    return lax.rem(y + rel[0], 2) * Z + lax.rem(z + sign * rel[1] + Z, Z)


def grp_at(step, sign):
    return lax.rem(lax.axis_index("grp") + sign * step + 16, 16)


def remote(src, dst, sems, n, axis, where):
    return remote_to(src, dst, sems, n, {axis: where})


def remote_to(src, dst, sems, n, device):
    return pltpu.make_async_remote_copy(
        src_ref=src,
        dst_ref=dst,
        send_sem=sems.at[0, n],
        recv_sem=sems.at[1, n],
        device_id=device,
        device_id_type=MESH,
    )


def start_all(copies):
    for c in copies:
        c.start()
    return copies


def kernel(
    amp_hbm, fac_hbm, chg_hbm, occ_e_hbm, vir_e_hbm, occ_n_hbm, vir_n_hbm, atoms_hbm, pos_hbm,
    refined_ref, block_ref,
    amp_ref, chg_ref, occ_e, vir_e, occ_n, vir_n, atoms_ref, pos_ref,
    fac, amp_z, amp_yz, part_y, land_y, part_z, land_z,
    e_send, e_land, c_send, c_land, g_send, g_row, p_land, g_land, x_send, x_land, pos8, k_hi, k_lo,
    in_sem, fac_sem, az_sem, ayz_sem, py_sem, pz_sem, e_sem, c_sem, p_sem, g_sem, x_sem,
):
    me = lax.axis_index("inner")
    grp = lax.axis_index("grp")
    rows_n, pairs = amp_ref.shape
    segs = pairs // NVIR
    aux, tiles = fac_hbm.shape[:2]
    per = pairs // 128

    barrier = pltpu.get_barrier_semaphore()
    for rel in [(1, 0)] + [(0, dz) for dz in NEAR_Z]:
        pl.semaphore_signal(barrier, inc=1, device_id={"inner": inner_at(rel, 1)}, device_id_type=MESH)
    for a in range(1, 16):
        pl.semaphore_signal(barrier, inc=1, device_id={"grp": grp_at(a, 1)}, device_id_type=MESH)
    pairs_in = [
        (amp_hbm, amp_ref), (vir_e_hbm, vir_e), (occ_e_hbm, occ_e), (occ_n_hbm, occ_n),
        (vir_n_hbm, vir_n), (atoms_hbm, atoms_ref), (pos_hbm, pos_ref), (chg_hbm, chg_ref),
    ]
    inputs = start_all(
        [pltpu.make_async_copy(src, dst, in_sem.at[n]) for n, (src, dst) in enumerate(pairs_in)]
    )
    inputs[0].wait()
    pl.semaphore_wait(barrier, 1 + len(NEAR_Z) + N_GRP)

    along, across = {}, {}

    def send_along(src, dz, at):
        n = ARRIVALS.index(at)
        along[at] = remote(src, amp_z.at[n], az_sem, n, "inner", inner_at((0, dz), 1))
        along[at].start()

    def send_across(src, at):
        n = ARRIVALS.index(at) + 1 if at else 0
        across[at] = remote(src, amp_yz.at[n], ayz_sem, n, "inner", inner_at((1, 0), 1))
        across[at].start()

    send_across(amp_ref, 0)
    for dz in NEAR_Z:
        send_along(amp_ref, dz, dz)
    loads = []
    for n, rel in enumerate(ORDER):
        for m in range(per):
            j = inner_at(rel, -1) * per + m
            loads.append(
                pltpu.make_async_copy(
                    fac_hbm.at[:, j], fac.at[j, pl.ds(0, aux)], fac_sem.at[n // GROUP]
                )
            )
            loads[-1].start()
    for copy in inputs[1:]:
        copy.wait()

    pos8[...] = jnp.zeros_like(pos8)
    pos8[0:3, :] = pos_ref[...]
    p_all = pos8[...]
    p_hi = p_all.astype(jnp.bfloat16).astype(jnp.float32)
    p_mid = (p_all - p_hi).astype(jnp.bfloat16).astype(jnp.float32)
    p_lo = p_all - p_hi - p_mid
    hot = (
        (lax.broadcasted_iota(jnp.int32, (pos_ref.shape[1], 128), 0) == atoms_ref[...])
        .astype(jnp.float32)
        .astype(jnp.bfloat16)
    )
    xyz3 = dot(jnp.concatenate([p_hi, p_mid, p_lo], axis=0).astype(jnp.bfloat16), hot, NN)
    own_xyz = xyz3[0:8] + xyz3[8:16] + xyz3[16:24]
    x_send[...] = own_xyz

    for at, step, then in RELAYED:
        along[at].wait_recv()
        shard = amp_z.at[ARRIVALS.index(at)]
        send_along(shard, step, then)
        send_across(shard, at)
    along[6].wait_recv()
    send_across(amp_z.at[ARRIVALS.index(6)], 6)
    x_copies = start_all(
        [remote(x_send, x_land.at[a - 1], x_sem, a - 1, "grp", grp_at(a, 1)) for a in range(1, 16)]
    )
    lane = lax.broadcasted_iota(jnp.int32, (STATES, pairs), 1)
    seg, vir = lane // NVIR, lane % NVIR
    vir_in = [vir < vir_n[c] for c in range(2)]

    def active_of(who):
        return jnp.concatenate(
            [jnp.where(vir_in[c] & (seg + who * segs < occ_n[c]), 1.0, 0.0) for c in range(2)],
            axis=0,
        )

    active = active_of(me)
    gap = jnp.concatenate(
        [
            jnp.concatenate(
                [
                    jnp.broadcast_to(vir_e[c : c + 1, :] - occ_e[c, me * segs + m], (STATES, NVIR))
                    for m in range(segs)
                ],
                axis=1,
            )
            for c in range(2)
        ],
        axis=0,
    )
    masked = amp_ref[...].astype(jnp.float32) * active
    own_num = jnp.sum(gap * masked * masked, axis=1, keepdims=True)
    own_sq = jnp.sum(masked * masked, axis=1, keepdims=True)
    for j in range(tiles):
        fac[j, aux:128] = jnp.zeros((128 - aux, 2, 128), jnp.bfloat16)
    flat = fac.reshape(tiles, 256, 128)

    def piece(who):
        return jnp.concatenate([flat[who * per + m] for m in range(per)], axis=1)

    def loaded(group):
        for c in loads[group * GROUP * per : (group + 1) * GROUP * per]:
            c.wait()

    def fit(amps, rel):
        n, who = ORDER.index(rel), inner_at(rel, -1)
        if n % GROUP == 0:
            loaded(n // GROUP)
        theirs = (amps.astype(jnp.float32) * active_of(who)).astype(jnp.bfloat16)
        return dot(theirs, piece(who), NT)

    def fit_along(at):
        return fit(amp_z[ARRIVALS.index(at)], (0, at))

    def fit_across(at):
        across[at].wait_recv()
        return fit(amp_yz[ARRIVALS.index(at) + 1 if at else 0], (1, at))

    loaded(0)
    fitted = dot(masked.astype(jnp.bfloat16), piece(me), NT) + fit_along(1) + fit_along(7)
    for at in (3, 5, 4):
        along[at].wait_recv()
        send_across(amp_z.at[ARRIVALS.index(at)], at)
    for at in (2, 6, 3, 5, 4):
        fitted = fitted + fit_along(at)
    for at in (0,) + ARRIVALS:
        fitted = fitted + fit_across(at)
    parity = lax.broadcasted_iota(jnp.int32, fitted.shape, 1) % 2
    monomer = lax.broadcasted_iota(jnp.int32, fitted.shape, 0) // STATES
    fitted = jnp.where(parity == monomer, fitted, 0.0)
    low = fitted.astype(jnp.bfloat16)

    order = FAR_Z + (0,)
    cross = []
    for n, dz in enumerate(order):
        part_y[n] = (2.0 * dot(low, piece(inner_at((1, dz), 1)), NN)).astype(jnp.bfloat16)
        cross.append(remote(part_y.at[n], land_y.at[n], py_sem, n, "inner", inner_at((1, 0), 1)))
        cross[-1].start()

    row16 = lax.broadcasted_iota(jnp.int32, (rows_n, 128), 0)
    lane16 = lax.broadcasted_iota(jnp.int32, (rows_n, 128), 1)
    num = own_num + 2.0 * jnp.sum(low.astype(jnp.float32) * fitted, axis=1, keepdims=True)
    tile = jnp.where(lane16 == row16, num, 0.0) + jnp.where(lane16 == row16 + 16, own_sq, 0.0)
    e_row = jnp.sum(tile, axis=0, keepdims=True)
    e_send[...] = e_row
    e_copies = start_all(
        [
            remote(e_send, e_land.at[n], e_sem, n, "inner", inner_at(rel, 1))
            for n, rel in enumerate(PEERS)
        ]
    )

    down = []
    for n, dz in enumerate(order):
        own = 2.0 * dot(low, piece(inner_at((0, dz), 1)), NN)
        cross[n].wait_recv()
        own = own + land_y[n].astype(jnp.float32)
        if dz:
            part_z[n] = own.astype(jnp.bfloat16)
            down.append(remote(part_z.at[n], land_z.at[n], pz_sem, n, "inner", inner_at((0, dz), 1)))
            down[-1].start()
    coulomb = own

    own_cols = jnp.transpose(own_xyz)
    for a in range(16):
        if a > 0:
            x_copies[a - 1].wait_recv()
        there = own_xyz if a == 0 else x_land[a - 1]
        r2 = jnp.zeros((128, 128), jnp.float32)
        for k in range(3):
            d = own_cols[:, k : k + 1] - there[k : k + 1, :]
            r2 = r2 + d * d
        hi, lo = split(lax.rsqrt(r2 + 1.0))
        k_hi[:, a * 128 : (a + 1) * 128] = hi
        k_lo[:, a * 128 : (a + 1) * 128] = lo

    for copy in e_copies:
        copy.wait_recv()
    total = e_row
    for n in range(N_IN):
        total = total + e_land[n]
    num = jnp.sum(jnp.where(lane16 == row16, total, 0.0), axis=1, keepdims=True)
    sq = jnp.sum(jnp.where(lane16 == row16 + 16, total, 0.0), axis=1, keepdims=True)
    energy = num / (sq + EPSILON)

    for n in reversed(range(N_Z)):
        down[n].wait_recv()
        coulomb = coulomb + land_z[n].astype(jnp.float32)

    sigma = gap * masked + active * coulomb
    refined = active * (masked - (sigma - energy * masked) / gap)
    refined_ref[...] = refined
    both = dot(refined.astype(jnp.bfloat16), chg_ref[...], NT)
    first = lane16[0:STATES] < 64
    own = jnp.where(first, both[0:STATES], both[STATES:])
    c_send[...] = own
    c_copies = start_all(
        [
            remote(c_send, c_land.at[n], c_sem, n, "inner", inner_at((0, dz), 1))
            for n, dz in enumerate(FAR_Z)
        ]
    )
    charges = own
    for n in reversed(range(N_Z)):
        c_copies[n].wait_recv()
        charges = charges + c_land[n]
    g_send[...] = charges
    g_row[...] = g_send[pl.ds(lax.rem(me, STATES), 1), :]
    p_copy = remote(g_send, p_land, p_sem, 0, "inner", inner_at((1, 0), 1))
    p_copy.start()
    g_copies = start_all(
        [
            remote_to(
                g_row, g_land.at[n], g_sem, n,
                {"grp": grp_at(a, 1), "inner": inner_at((dy, 0), 1)},
            )
            for n, (dy, a) in enumerate(CROWD)
        ]
    )
    p_copy.wait_recv()
    p_row = p_land[pl.ds(lax.rem(me, STATES), 1), :]
    charges = charges + p_land[...]

    rows = jnp.concatenate([jnp.where(first, charges, 0.0), jnp.where(first, 0.0, charges)], axis=0)
    rows_hi, rows_lo = split(rows)
    with_hi = dot(jnp.concatenate([rows_hi, rows_lo], axis=0), k_hi[...], NN)
    field = with_hi[0:16] + with_hi[16:32] + dot(rows_hi, k_lo[...], NN)

    t = lax.rem(me, STATES)
    half = me // STATES
    in_half = (lax.broadcasted_iota(jnp.int32, (1, 128), 1) // 64) == half
    out_lane = lax.broadcasted_iota(jnp.int32, (16, 16), 1)
    out_row = lax.broadcasted_iota(jnp.int32, (16, 16), 0)
    for copies in (along.values(), across.values(), x_copies, cross, e_copies, down, c_copies):
        for c in copies:
            c.wait_send()
    p_copy.wait_send()
    block = jnp.zeros((16, 16), jnp.float32)
    for a in range(16):
        if a > 0:
            g_copies[a - 1].wait_recv()
            g_copies[a - 1 + N_GRP].wait_recv()
            q = g_land[a - 1] + g_land[a - 1 + N_GRP]
        else:
            q = g_row[...] + p_row
        q = jnp.where(in_half, q, 0.0)
        column = jnp.sum(field[:, a * 128 : (a + 1) * 128] * q, axis=1, keepdims=True)
        block = jnp.where(out_lane == grp_at(a, -1), column, block)
    same = (out_lane == grp) & (out_row // STATES == half)
    block_ref[...] = jnp.where(same, jnp.where(out_row % STATES == t, energy, 0.0), block)
    for c in g_copies:
        c.wait_send()


def hand_over(refined_ref, block_ref, refined_hbm, block_hbm, rows, sems):
    big = pltpu.make_async_copy(refined_ref, refined_hbm, sems.at[0])
    big.start()
    for r in range(block_ref.shape[0]):
        rows[r] = block_ref[r : r + 1, :]
    small = pltpu.make_async_copy(rows, block_hbm, sems.at[1])
    small.start()
    big.wait()
    small.wait()


def local(
    amplitudes, factors, atom_charges, eps_occ, eps_vir, occ_count, vir_count, atom_list, positions
):
    monomers, states, pairs = amplitudes.shape
    aux, every = factors.shape[1:]
    rows = monomers * states
    vmem = pl.BlockSpec(memory_space=pltpu.VMEM)
    hbm = pl.BlockSpec(memory_space=pl.ANY)
    bf, f32, i32 = jnp.bfloat16, jnp.float32, jnp.int32
    by_tile = jnp.transpose(factors, (1, 0, 2)).reshape(aux, monomers, every // 128, 128)
    sem = pltpu.SemaphoreType.DMA
    refined, block = pl.pallas_call(
        kernel,
        name="exciton",
        out_shape=(
            pltpu.VMEM((rows, pairs), f32),
            pltpu.VMEM((rows, rows), f32),
        ),
        in_specs=[hbm] * 9,
        out_specs=(vmem, vmem),
        scratch_shapes=[
            pltpu.VMEM((rows, pairs), bf),
            pltpu.VMEM((monomers * 64, pairs), bf),
            pltpu.SMEM(eps_occ.shape, f32),
            pltpu.VMEM(eps_vir.shape, f32),
            pltpu.SMEM(occ_count.shape, i32),
            pltpu.SMEM(vir_count.shape, i32),
            pltpu.VMEM((1, 128), i32),
            pltpu.VMEM(positions.shape, f32),
            pltpu.VMEM((every // 128, 128, monomers, 128), bf),
            pltpu.VMEM((N_Z, rows, pairs), bf),
            pltpu.VMEM((Z, rows, pairs), bf),
            pltpu.VMEM((Z, rows, pairs), bf),
            pltpu.VMEM((Z, rows, pairs), bf),
            pltpu.VMEM((N_Z, rows, pairs), bf),
            pltpu.VMEM((N_Z, rows, pairs), bf),
            pltpu.VMEM((1, 128), f32),
            pltpu.VMEM((N_IN, 1, 128), f32),
            pltpu.VMEM((8, 128), f32),
            pltpu.VMEM((N_Z, 8, 128), f32),
            pltpu.VMEM((8, 128), f32),
            pltpu.VMEM((1, 128), f32),
            pltpu.VMEM((8, 128), f32),
            pltpu.VMEM((2 * N_GRP, 1, 128), f32),
            pltpu.VMEM((8, 128), f32),
            pltpu.VMEM((N_GRP, 8, 128), f32),
            pltpu.VMEM((8, positions.shape[1]), f32),
            pltpu.VMEM((128, 2048), bf),
            pltpu.VMEM((128, 2048), bf),
            sem((8,)),
            sem((4,)),
            sem((2, N_Z)),
            sem((2, Z)),
            sem((2, Z)),
            sem((2, N_Z)),
            sem((2, N_IN)),
            sem((2, N_Z)),
            sem((2, 1)),
            sem((2, 2 * N_GRP)),
            sem((2, N_GRP)),
        ],
        compiler_params=pltpu.CompilerParams(collective_id=0, has_side_effects=True),
    )(
        amplitudes.reshape(rows, pairs),
        by_tile.transpose(0, 2, 1, 3),
        atom_charges.reshape(monomers * 64, pairs),
        eps_occ, eps_vir, occ_count, vir_count, atom_list.reshape(1, -1), positions,
    )
    refined, block = pl.pallas_call(
        hand_over,
        name="hand_over",
        out_shape=(
            jax.ShapeDtypeStruct((rows, pairs), f32),
            jax.ShapeDtypeStruct((rows, 1, rows), f32),
        ),
        in_specs=[vmem, vmem],
        out_specs=(hbm, hbm),
        scratch_shapes=[pltpu.VMEM((rows, 1, rows), f32), sem((2,))],
    )(*(pltpu.with_memory_space_constraint(a, pltpu.VMEM) for a in (refined, block)))
    return refined.reshape(monomers, states, pairs), jnp.swapaxes(block, 1, 2)


def solution(mesh):
    in_specs = (
        P("grp", None, "inner"),
        P("grp", "inner", None),
        P("grp", None, "inner"),
        P("grp", None),
        P("grp", None),
        P("grp"),
        P("grp"),
        P("grp"),
        P(),
    )
    out_specs = (P("grp", None, "inner"), P("grp", None, "inner"))
    return jax.shard_map(local, mesh=mesh, in_specs=in_specs, out_specs=out_specs, check_vma=False)
```

```python
import jax
import jax.numpy as jnp
from jax import lax
from jax.experimental import pallas as pl
from jax.experimental.pallas import tpu as pltpu
from jax.sharding import PartitionSpec as P

NVIR = 256
STATES = 8
EPSILON = 1e-06
Z = 8
MESH = pl.DeviceIdType.MESH
FAR_Z = (4, 3, 5, 2, 6, 1, 7)
NEAR_Z = (1, 7, 2, 6)
RELAYED = ((1, 2, 3), (7, 6, 5), (2, 2, 4))
ARRIVALS = (1, 7, 2, 6, 3, 5, 4)
ORDER = [(dy, dz) for dy in (0, 1) for dz in (0,) + ARRIVALS]
GROUP = 4
PEERS = sorted(
    [(dy, dz) for dy in (0, 1) for dz in range(Z) if (dy, dz) != (0, 0)],
    key=lambda r: -(2 * r[0] + min(r[1], Z - r[1])),
)
N_IN = len(PEERS)
N_Z = len(FAR_Z)
CROWD = [(dy, a) for dy in (1, 0) for a in range(1, 16)]
N_GRP = 15
NT = (((1,), (1,)), ((), ()))
NN = (((1,), (0,)), ((), ()))


def split(x):
    high = x.astype(jnp.bfloat16)
    return high, (x - high.astype(jnp.float32)).astype(jnp.bfloat16)


def dot(a, b, dims):
    return lax.dot_general(a, b, dims, preferred_element_type=jnp.float32)


def inner_at(rel, sign):
    me = lax.axis_index("inner")
    turn = sign * (1 - 2 * lax.rem(lax.axis_index("grp"), 2))
    y, z = me // Z, me % Z
    return lax.rem(y + rel[0], 2) * Z + lax.rem(z + turn * rel[1] + Z, Z)


def grp_at(step, sign):
    return lax.rem(lax.axis_index("grp") + sign * step + 16, 16)


def remote(src, dst, sems, n, axis, where):
    return remote_to(src, dst, sems, n, {axis: where})


def remote_to(src, dst, sems, n, device):
    return pltpu.make_async_remote_copy(
        src_ref=src,
        dst_ref=dst,
        send_sem=sems.at[0, n],
        recv_sem=sems.at[1, n],
        device_id=device,
        device_id_type=MESH,
    )


def start_all(copies):
    for c in copies:
        c.start()
    return copies


def kernel(
    amp_hbm, fac_hbm, chg_hbm, occ_e_hbm, vir_e_hbm, occ_n_hbm, vir_n_hbm, atoms_hbm, pos_hbm,
    refined_ref, block_ref,
    amp_ref, chg_ref, occ_e, vir_e, occ_n, vir_n, atoms_ref, pos_ref,
    fac, amp_z, amp_yz, part_y, land_y, part_z, land_z,
    e_send, e_land, c_send, c_land, g_send, g_row, p_land, g_land, x_send, x_land, pos8, k_hi, k_lo,
    in_sem, fac_sem, az_sem, ayz_sem, py_sem, pz_sem, e_sem, c_sem, p_sem, g_sem, x_sem,
):
    me = lax.axis_index("inner")
    grp = lax.axis_index("grp")
    rows_n, pairs = amp_ref.shape
    segs = pairs // NVIR
    aux, tiles = fac_hbm.shape[:2]
    per = pairs // 128

    barrier = pltpu.get_barrier_semaphore()
    for rel in [(1, 0)] + [(0, dz) for dz in NEAR_Z]:
        pl.semaphore_signal(barrier, inc=1, device_id={"inner": inner_at(rel, 1)}, device_id_type=MESH)
    for a in range(1, 16):
        pl.semaphore_signal(barrier, inc=1, device_id={"grp": grp_at(a, 1)}, device_id_type=MESH)
    pairs_in = [
        (amp_hbm, amp_ref), (vir_e_hbm, vir_e), (occ_e_hbm, occ_e), (occ_n_hbm, occ_n),
        (vir_n_hbm, vir_n), (atoms_hbm, atoms_ref), (pos_hbm, pos_ref), (chg_hbm, chg_ref),
    ]
    inputs = start_all(
        [pltpu.make_async_copy(src, dst, in_sem.at[n]) for n, (src, dst) in enumerate(pairs_in)]
    )
    inputs[0].wait()
    pl.semaphore_wait(barrier, 1 + len(NEAR_Z) + N_GRP)

    along, across = {}, {}

    def send_along(src, dz, at):
        n = ARRIVALS.index(at)
        along[at] = remote(src, amp_z.at[n], az_sem, n, "inner", inner_at((0, dz), 1))
        along[at].start()

    def send_across(src, at):
        n = ARRIVALS.index(at) + 1 if at else 0
        across[at] = remote(src, amp_yz.at[n], ayz_sem, n, "inner", inner_at((1, 0), 1))
        across[at].start()

    send_across(amp_ref, 0)
    for dz in NEAR_Z:
        send_along(amp_ref, dz, dz)
    loads = []
    for n, rel in enumerate(ORDER):
        for m in range(per):
            j = inner_at(rel, -1) * per + m
            loads.append(
                pltpu.make_async_copy(
                    fac_hbm.at[:, j], fac.at[j, pl.ds(0, aux)], fac_sem.at[n // GROUP]
                )
            )
            loads[-1].start()
    for copy in inputs[1:]:
        copy.wait()

    pos8[...] = jnp.zeros_like(pos8)
    pos8[0:3, :] = pos_ref[...]
    p_all = pos8[...]
    p_hi = p_all.astype(jnp.bfloat16).astype(jnp.float32)
    p_mid = (p_all - p_hi).astype(jnp.bfloat16).astype(jnp.float32)
    p_lo = p_all - p_hi - p_mid
    hot = (
        (lax.broadcasted_iota(jnp.int32, (pos_ref.shape[1], 128), 0) == atoms_ref[...])
        .astype(jnp.float32)
        .astype(jnp.bfloat16)
    )
    xyz3 = dot(jnp.concatenate([p_hi, p_mid, p_lo], axis=0).astype(jnp.bfloat16), hot, NN)
    own_xyz = xyz3[0:8] + xyz3[8:16] + xyz3[16:24]
    x_send[...] = own_xyz

    for at, step, then in RELAYED:
        along[at].wait_recv()
        shard = amp_z.at[ARRIVALS.index(at)]
        send_along(shard, step, then)
        send_across(shard, at)
    along[6].wait_recv()
    send_across(amp_z.at[ARRIVALS.index(6)], 6)
    x_copies = start_all(
        [remote(x_send, x_land.at[a - 1], x_sem, a - 1, "grp", grp_at(a, 1)) for a in range(1, 16)]
    )
    lane = lax.broadcasted_iota(jnp.int32, (STATES, pairs), 1)
    seg, vir = lane // NVIR, lane % NVIR
    vir_in = [vir < vir_n[c] for c in range(2)]

    def active_of(who):
        return jnp.concatenate(
            [jnp.where(vir_in[c] & (seg + who * segs < occ_n[c]), 1.0, 0.0) for c in range(2)],
            axis=0,
        )

    active = active_of(me)
    gap = jnp.concatenate(
        [
            jnp.concatenate(
                [
                    jnp.broadcast_to(vir_e[c : c + 1, :] - occ_e[c, me * segs + m], (STATES, NVIR))
                    for m in range(segs)
                ],
                axis=1,
            )
            for c in range(2)
        ],
        axis=0,
    )
    masked = amp_ref[...].astype(jnp.float32) * active
    own_num = jnp.sum(gap * masked * masked, axis=1, keepdims=True)
    own_sq = jnp.sum(masked * masked, axis=1, keepdims=True)
    for j in range(tiles):
        fac[j, aux:128] = jnp.zeros((128 - aux, 2, 128), jnp.bfloat16)
    flat = fac.reshape(tiles, 256, 128)

    def piece(who):
        return jnp.concatenate([flat[who * per + m] for m in range(per)], axis=1)

    def loaded(group):
        for c in loads[group * GROUP * per : (group + 1) * GROUP * per]:
            c.wait()

    def fit(amps, rel):
        n, who = ORDER.index(rel), inner_at(rel, -1)
        if n % GROUP == 0:
            loaded(n // GROUP)
        theirs = (amps.astype(jnp.float32) * active_of(who)).astype(jnp.bfloat16)
        return dot(theirs, piece(who), NT)

    def fit_along(at):
        return fit(amp_z[ARRIVALS.index(at)], (0, at))

    def fit_across(at):
        across[at].wait_recv()
        return fit(amp_yz[ARRIVALS.index(at) + 1 if at else 0], (1, at))

    loaded(0)
    fitted = dot(masked.astype(jnp.bfloat16), piece(me), NT) + fit_along(1) + fit_along(7)
    for at in (3, 5, 4):
        along[at].wait_recv()
        send_across(amp_z.at[ARRIVALS.index(at)], at)
    for at in (2, 6, 3, 5, 4):
        fitted = fitted + fit_along(at)
    for at in (0,) + ARRIVALS:
        fitted = fitted + fit_across(at)
    parity = lax.broadcasted_iota(jnp.int32, fitted.shape, 1) % 2
    monomer = lax.broadcasted_iota(jnp.int32, fitted.shape, 0) // STATES
    fitted = jnp.where(parity == monomer, fitted, 0.0)
    low = fitted.astype(jnp.bfloat16)

    order = FAR_Z + (0,)
    cross = []
    for n, dz in enumerate(order):
        part_y[n] = (2.0 * dot(low, piece(inner_at((1, dz), 1)), NN)).astype(jnp.bfloat16)
        cross.append(remote(part_y.at[n], land_y.at[n], py_sem, n, "inner", inner_at((1, 0), 1)))
        cross[-1].start()

    row16 = lax.broadcasted_iota(jnp.int32, (rows_n, 128), 0)
    lane16 = lax.broadcasted_iota(jnp.int32, (rows_n, 128), 1)
    num = own_num + 2.0 * jnp.sum(low.astype(jnp.float32) * fitted, axis=1, keepdims=True)
    tile = jnp.where(lane16 == row16, num, 0.0) + jnp.where(lane16 == row16 + 16, own_sq, 0.0)
    e_row = jnp.sum(tile, axis=0, keepdims=True)
    e_send[...] = e_row
    e_copies = start_all(
        [
            remote(e_send, e_land.at[n], e_sem, n, "inner", inner_at(rel, 1))
            for n, rel in enumerate(PEERS)
        ]
    )

    down = []
    for n, dz in enumerate(order):
        own = 2.0 * dot(low, piece(inner_at((0, dz), 1)), NN)
        cross[n].wait_recv()
        own = own + land_y[n].astype(jnp.float32)
        if dz:
            part_z[n] = own.astype(jnp.bfloat16)
            down.append(remote(part_z.at[n], land_z.at[n], pz_sem, n, "inner", inner_at((0, dz), 1)))
            down[-1].start()
    coulomb = own

    own_cols = jnp.transpose(own_xyz)
    for a in range(16):
        if a > 0:
            x_copies[a - 1].wait_recv()
        there = own_xyz if a == 0 else x_land[a - 1]
        r2 = jnp.zeros((128, 128), jnp.float32)
        for k in range(3):
            d = own_cols[:, k : k + 1] - there[k : k + 1, :]
            r2 = r2 + d * d
        hi, lo = split(lax.rsqrt(r2 + 1.0))
        k_hi[:, a * 128 : (a + 1) * 128] = hi
        k_lo[:, a * 128 : (a + 1) * 128] = lo

    for copy in e_copies:
        copy.wait_recv()
    total = e_row
    for n in range(N_IN):
        total = total + e_land[n]
    num = jnp.sum(jnp.where(lane16 == row16, total, 0.0), axis=1, keepdims=True)
    sq = jnp.sum(jnp.where(lane16 == row16 + 16, total, 0.0), axis=1, keepdims=True)
    energy = num / (sq + EPSILON)

    for n in reversed(range(N_Z)):
        down[n].wait_recv()
        coulomb = coulomb + land_z[n].astype(jnp.float32)

    sigma = gap * masked + active * coulomb
    refined = active * (masked - (sigma - energy * masked) / gap)
    refined_ref[...] = refined
    both = dot(refined.astype(jnp.bfloat16), chg_ref[...], NT)
    first = lane16[0:STATES] < 64
    own = jnp.where(first, both[0:STATES], both[STATES:])
    c_send[...] = own
    c_copies = start_all(
        [
            remote(c_send, c_land.at[n], c_sem, n, "inner", inner_at((0, dz), 1))
            for n, dz in enumerate(FAR_Z)
        ]
    )
    charges = own
    for n in reversed(range(N_Z)):
        c_copies[n].wait_recv()
        charges = charges + c_land[n]
    g_send[...] = charges
    g_row[...] = g_send[pl.ds(lax.rem(me, STATES), 1), :]
    p_copy = remote(g_send, p_land, p_sem, 0, "inner", inner_at((1, 0), 1))
    p_copy.start()
    g_copies = start_all(
        [
            remote_to(
                g_row, g_land.at[n], g_sem, n,
                {"grp": grp_at(a, 1), "inner": inner_at((dy, 0), 1)},
            )
            for n, (dy, a) in enumerate(CROWD)
        ]
    )
    p_copy.wait_recv()
    p_row = p_land[pl.ds(lax.rem(me, STATES), 1), :]
    charges = charges + p_land[...]

    rows = jnp.concatenate([jnp.where(first, charges, 0.0), jnp.where(first, 0.0, charges)], axis=0)
    rows_hi, rows_lo = split(rows)
    with_hi = dot(jnp.concatenate([rows_hi, rows_lo], axis=0), k_hi[...], NN)
    field = with_hi[0:16] + with_hi[16:32] + dot(rows_hi, k_lo[...], NN)

    t = lax.rem(me, STATES)
    half = me // STATES
    in_half = (lax.broadcasted_iota(jnp.int32, (1, 128), 1) // 64) == half
    out_lane = lax.broadcasted_iota(jnp.int32, (16, 16), 1)
    out_row = lax.broadcasted_iota(jnp.int32, (16, 16), 0)
    for copies in (along.values(), across.values(), x_copies, cross, e_copies, down, c_copies):
        for c in copies:
            c.wait_send()
    p_copy.wait_send()
    block = jnp.zeros((16, 16), jnp.float32)
    for a in range(16):
        if a > 0:
            g_copies[a - 1].wait_recv()
            g_copies[a - 1 + N_GRP].wait_recv()
            q = g_land[a - 1] + g_land[a - 1 + N_GRP]
        else:
            q = g_row[...] + p_row
        q = jnp.where(in_half, q, 0.0)
        column = jnp.sum(field[:, a * 128 : (a + 1) * 128] * q, axis=1, keepdims=True)
        block = jnp.where(out_lane == grp_at(a, -1), column, block)
    same = (out_lane == grp) & (out_row // STATES == half)
    block_ref[...] = jnp.where(same, jnp.where(out_row % STATES == t, energy, 0.0), block)
    for c in g_copies:
        c.wait_send()


def hand_over(refined_ref, block_ref, refined_hbm, block_hbm, rows, sems):
    big = pltpu.make_async_copy(refined_ref, refined_hbm, sems.at[0])
    big.start()
    for r in range(block_ref.shape[0]):
        rows[r] = block_ref[r : r + 1, :]
    small = pltpu.make_async_copy(rows, block_hbm, sems.at[1])
    small.start()
    big.wait()
    small.wait()


def local(
    amplitudes, factors, atom_charges, eps_occ, eps_vir, occ_count, vir_count, atom_list, positions
):
    monomers, states, pairs = amplitudes.shape
    aux, every = factors.shape[1:]
    rows = monomers * states
    vmem = pl.BlockSpec(memory_space=pltpu.VMEM)
    hbm = pl.BlockSpec(memory_space=pl.ANY)
    bf, f32, i32 = jnp.bfloat16, jnp.float32, jnp.int32
    by_tile = jnp.transpose(factors, (1, 0, 2)).reshape(aux, monomers, every // 128, 128)
    sem = pltpu.SemaphoreType.DMA
    refined, block = pl.pallas_call(
        kernel,
        name="exciton",
        out_shape=(
            pltpu.VMEM((rows, pairs), f32),
            pltpu.VMEM((rows, rows), f32),
        ),
        in_specs=[hbm] * 9,
        out_specs=(vmem, vmem),
        scratch_shapes=[
            pltpu.VMEM((rows, pairs), bf),
            pltpu.VMEM((monomers * 64, pairs), bf),
            pltpu.SMEM(eps_occ.shape, f32),
            pltpu.VMEM(eps_vir.shape, f32),
            pltpu.SMEM(occ_count.shape, i32),
            pltpu.SMEM(vir_count.shape, i32),
            pltpu.VMEM((1, 128), i32),
            pltpu.VMEM(positions.shape, f32),
            pltpu.VMEM((every // 128, 128, monomers, 128), bf),
            pltpu.VMEM((N_Z, rows, pairs), bf),
            pltpu.VMEM((Z, rows, pairs), bf),
            pltpu.VMEM((Z, rows, pairs), bf),
            pltpu.VMEM((Z, rows, pairs), bf),
            pltpu.VMEM((N_Z, rows, pairs), bf),
            pltpu.VMEM((N_Z, rows, pairs), bf),
            pltpu.VMEM((1, 128), f32),
            pltpu.VMEM((N_IN, 1, 128), f32),
            pltpu.VMEM((8, 128), f32),
            pltpu.VMEM((N_Z, 8, 128), f32),
            pltpu.VMEM((8, 128), f32),
            pltpu.VMEM((1, 128), f32),
            pltpu.VMEM((8, 128), f32),
            pltpu.VMEM((2 * N_GRP, 1, 128), f32),
            pltpu.VMEM((8, 128), f32),
            pltpu.VMEM((N_GRP, 8, 128), f32),
            pltpu.VMEM((8, positions.shape[1]), f32),
            pltpu.VMEM((128, 2048), bf),
            pltpu.VMEM((128, 2048), bf),
            sem((8,)),
            sem((4,)),
            sem((2, N_Z)),
            sem((2, Z)),
            sem((2, Z)),
            sem((2, N_Z)),
            sem((2, N_IN)),
            sem((2, N_Z)),
            sem((2, 1)),
            sem((2, 2 * N_GRP)),
            sem((2, N_GRP)),
        ],
        compiler_params=pltpu.CompilerParams(collective_id=0, has_side_effects=True),
    )(
        amplitudes.reshape(rows, pairs),
        by_tile.transpose(0, 2, 1, 3),
        atom_charges.reshape(monomers * 64, pairs),
        eps_occ, eps_vir, occ_count, vir_count, atom_list.reshape(1, -1), positions,
    )
    refined, block = pl.pallas_call(
        hand_over,
        name="hand_over",
        out_shape=(
            jax.ShapeDtypeStruct((rows, pairs), f32),
            jax.ShapeDtypeStruct((rows, 1, rows), f32),
        ),
        in_specs=[vmem, vmem],
        out_specs=(hbm, hbm),
        scratch_shapes=[pltpu.VMEM((rows, 1, rows), f32), sem((2,))],
    )(*(pltpu.with_memory_space_constraint(a, pltpu.VMEM) for a in (refined, block)))
    return refined.reshape(monomers, states, pairs), jnp.swapaxes(block, 1, 2)


def solution(mesh):
    in_specs = (
        P("grp", None, "inner"),
        P("grp", "inner", None),
        P("grp", None, "inner"),
        P("grp", None),
        P("grp", None),
        P("grp"),
        P("grp"),
        P("grp"),
        P(),
    )
    out_specs = (P("grp", None, "inner"), P("grp", None, "inner"))
    return jax.shard_map(local, mesh=mesh, in_specs=in_specs, out_specs=out_specs, check_vma=False)
```
